32 devices in a mesh: prow: 4 (over z), pcol: 8 (over y, x, core).
Axes of the slice: x: 2, y: 2, z: 4, core: 2. Of those that a mesh axis runs over, the one named last changes fastest.
Arguments:
- matrix: float32 [2048, 8192], P('prow', 'pcol'), may hold values from -6 to 6
- pivot_inverse: float32 [2, 512, 512], P(None, 'prow'), may hold values from -0.01171875 to 0.01171875
- row_live: int32 [2, 4], replicated, may hold values 0 or 1
- col_live: int32 [2, 16], replicated, may hold values 0 or 1
Outputs:
- factored: float32 [2048, 8192], P('prow', 'pcol')
The draws below stay inside these ranges and needn't reach their ends.
All inputs are finite; a program needn't handle non-finite values.
Results may differ from the reference program's by a relative error of at most 0.0001.
Values sent between devices are 32-bit elements; how exact they have to be, the bound alone decides.
A program may use at most 64 MiB of HBM per device.

```python
import jax
import jax.numpy as jnp
from jax import lax

B = 512
RB = 1
CB = 2
PANELS = 2
NBR = 4
NBC = 16
N_PROW = 4
N_PCOL = 8


def plant(result, key, least, high):
    shape = result.shape
    index_at = [jax.random.randint(jax.random.fold_in(key, axis), (), 0, shape[axis]) for axis in range(len(shape))]
    result = result.at[tuple(index_at)].set(least)
    longest = shape.index(max(shape))
    index_at[longest] = (index_at[longest] + 1) % shape[longest]
    return result.at[tuple(index_at)].set(high)


def levels(rng, dims, shards, least, high):
    def one(dim, shards_of):
        draws = jax.random.uniform(jax.random.fold_in(jax.random.fold_in(rng, 6), dim), (shards_of,), jnp.float32, least / len(shards), high / len(shards))
        return jnp.repeat(jnp.exp(draws), dims[dim] // shards_of).reshape((-1,) + (1,) * (len(dims) - dim - 1))

    level = one(*shards[0])
    for cut in shards[1:]:
        level = level * one(*cut)
    return level


def noise(rng, extent, deviation, bound, shards=(), held_as=jnp.bfloat16):
    values = deviation * jax.random.normal(rng, extent, jnp.float32)
    if shards:
        values = values * levels(rng, extent, shards, -0.22, 0.18)
    return jnp.clip(values, -bound, bound).astype(held_as)


def setup_inputs(seed: int = 0) -> dict:
    seeds = jax.random.split(jax.random.key(seed), 5)
    matrix = noise(seeds[0], (NBR * B, NBC * B), 1.0, 6.0, ((0, 4), (1, 8)), jnp.float32)
    pivot_inverse = noise(seeds[1], (PANELS, B, B), (B * B) ** -0.5, 0.01171875, ((1, 4),), jnp.float32)
    row_live = plant((jax.random.randint(seeds[2], (PANELS, NBR), 0, 4) < 3).astype(jnp.int32), jax.random.fold_in(seeds[2], 1), 0, 1)
    col_live = plant((jax.random.randint(seeds[3], (PANELS, NBC), 0, 4) < 3).astype(jnp.int32), jax.random.fold_in(seeds[3], 1), 0, 1)
    return dict(matrix=matrix, pivot_inverse=pivot_inverse, row_live=row_live, col_live=col_live)


def reference(matrix, pivot_inverse, row_live, col_live):
    block_rows = RB * N_PROW
    block_cols = CB * N_PCOL
    row_range = jnp.arange(block_rows, dtype=jnp.int32)
    col_range = jnp.arange(block_cols, dtype=jnp.int32)
    row_index = (row_range % RB) * N_PROW + row_range // RB
    col_index = (col_range % CB) * N_PCOL + col_range // CB
    for panel in range(PANELS):
        lower_mask = jnp.where(row_index > panel, jnp.take(row_live[panel], row_index), 0).astype(jnp.float32)
        upper_mask = jnp.where(col_index > panel, jnp.take(col_live[panel], col_index), 0).astype(jnp.float32)
        lower_mask = jnp.repeat(lower_mask, B)
        upper_mask = jnp.repeat(upper_mask, B)
        col_start = panel * CB * B
        row_start = panel * RB * B
        column_part = matrix[:, col_start:col_start + B]
        lower_part = jnp.dot(column_part, pivot_inverse[panel], precision=lax.Precision.HIGHEST) * lower_mask[:, None]
        upper_part = matrix[row_start:row_start + B, :] * upper_mask[None, :]
        matrix = matrix - jnp.dot(lower_part, upper_part, precision=lax.Precision.HIGHEST)
        keep_rows = jnp.repeat(row_index > panel, B)[:, None]
        matrix = matrix.at[:, col_start:col_start + B].set(jnp.where(keep_rows, lower_part, matrix[:, col_start:col_start + B]))
    return matrix
```

```python
import functools

import jax
import jax.numpy as jnp
from jax import lax
from jax.experimental import pallas as pl
from jax.experimental.pallas import tpu as pltpu
from jax.sharding import PartitionSpec as P

MESH = pl.DeviceIdType.MESH
CORES = 2
CHUNK = 256
PIECES = 8
TAIL = 4


def split(x):
    high = x.astype(jnp.bfloat16)
    return high, (x - high.astype(jnp.float32)).astype(jnp.bfloat16)


def product(left_high, left_low, right_high, right_low):
    dot = functools.partial(jnp.dot, preferred_element_type=jnp.float32)
    return dot(left_high, right_high) + (dot(left_high, right_low) + dot(left_low, right_high))


def kernel(
    n_row, n_col, row_live, col_live, mat, piv, out,
    acc, u, p, a, low, low_high, low_rest, u_high, u_rest,
    acc_sem, out_sem, u_send, u_recv, p_send, p_recv, p_pass, p_passed, p_own,
    a_own, a_send, a_recv, t_send, t_recv, l_send, l_recv, l_pass, l_passed,
):
    z, pcol = lax.axis_index("prow"), lax.axis_index("pcol")
    core, chip = lax.rem(pcol, CORES), lax.div(pcol, CORES)
    n_chip = n_col // CORES
    partner = (z, pcol + 1 - 2 * core)
    width, half = piv.shape[2], piv.shape[2] // CORES
    rows_own = piv.shape[1]
    rows_half = rows_own // CORES
    chunks, _, chunk = acc.shape
    per_block = width // chunk
    pieces = u_send.shape[1] // chunks
    piece = width // pieces
    steps = chunks * pieces
    last = n_row - 1
    first_chip, active, both = chip == 0, z > 0, z > 1

    def remote(src, dst, send, recv, to):
        return pltpu.make_async_remote_copy(
            src_ref=src, dst_ref=dst, send_sem=send, recv_sem=recv, device_id=to, device_id_type=MESH
        )

    def acc_load(j):
        return pltpu.make_async_copy(mat.at[:, pl.ds(j * chunk, chunk)], acc.at[j], acc_sem.at[j])

    def out_store(j):
        return pltpu.make_async_copy(acc.at[j], out.at[:, pl.ds(j * chunk, chunk)], out_sem.at[j])

    def pivot_own(k):
        return pltpu.make_async_copy(piv.at[k], p.at[k, pl.ds(z * rows_own, rows_own)], p_own.at[k])

    def pivot_rows(k, source):
        return p.at[k, pl.ds(pl.multiple_of(source * rows_own + core * rows_half, 8), rows_half)]

    def pivot_send(k, target):
        return remote(
            piv.at[k, pl.ds(pl.multiple_of(core * rows_half, 8), rows_half)],
            pivot_rows(k, z), p_send.at[k, target], p_recv.at[k, z], (target, pcol),
        )

    def pivot_landed(k, source):
        return remote(pivot_rows(k, source), pivot_rows(k, source), p_send.at[k, source], p_recv.at[k, source], (z, pcol))

    def pivot_pass(k, source):
        return remote(pivot_rows(k, source), pivot_rows(k, source), p_pass.at[k, source], p_passed.at[k, source], partner)

    def piece_of(ref, j, r):
        return ref.at[j, pl.ds(pl.multiple_of(r * piece, 8), piece)]

    def relay_copy(k, s):
        place = piece_of(u.at[k], s // pieces, s % pieces)
        return remote(place, place, u_send.at[k, s], u_recv.at[k, s], (z + 1, pcol))

    def origin_copy(k, s):
        j, r = s // pieces, s % pieces
        return remote(piece_of(acc, j, r), piece_of(u.at[k], j, r), u_send.at[k, s], u_recv.at[k, s], (z + 1, pcol))

    def start_of(k):
        return jnp.where(pcol <= k, per_block * pieces, 0)

    def relay(k, begin, end):
        def body(s, carry):
            copy = relay_copy(k, s)
            copy.wait_recv()

            @pl.when(z < last)
            def _():
                copy.start()

            return carry

        lax.fori_loop(jnp.maximum(begin, start_of(k)), end, body, 0)

    def originate(k, begin, end):
        def body(s, carry):
            origin_copy(k, s).start()
            return carry

        lax.fori_loop(jnp.maximum(begin, start_of(k)), end, body, 0)

    def finish_sends(k, copy):
        def body(s, carry):
            copy(k, s).wait_send()
            return carry

        lax.fori_loop(start_of(k), steps, body, 0)

    def own_rows():
        return pl.ds(pl.multiple_of(core * half, 8), half)

    def lower_send(k, target):
        rows = low.at[k, own_rows()]
        return remote(rows, rows, l_send.at[k, target], l_recv.at[k], (z, target * CORES + core))

    def lower_pass(k):
        rows = low.at[k, own_rows()]
        return remote(rows, rows, l_pass.at[k], l_passed.at[k], partner)

    def row_mask(k):
        return row_live[k, z].astype(jnp.float32)

    def gather_pivot(k):
        for source in range(n_row):
            @pl.when(z != source)
            def _():
                pivot_landed(k, source).wait_recv()
                pivot_pass(k, source).start()
        pivot_own(k).wait()
        for source in range(n_row):
            @pl.when(z != source)
            def _():
                pivot_pass(k, source).wait_recv()

    def apply_pivot(k, left):
        left_high, left_low = split(left)
        for q in range(per_block):
            columns = pl.ds(q * chunk, chunk)
            right = split(p[k, :, columns])
            low[k, own_rows(), columns] = row_mask(k) * product(left_high, left_low, *right)
        for target in range(n_chip - 1, 0, -1):
            lower_send(k, target).start()
        lower_pass(k).start()

    def take_lower(k):
        @pl.when(chip > 0)
        def _():
            lower_send(k, 0).wait_recv()
            lower_pass(k).start()

        lower_pass(k).wait_recv()
        low_high[k], low_rest[k] = split(low[k])

    def update(k, j):
        live = col_live[k, pcol + (j // per_block) * n_col].astype(jnp.float32)

        def run():
            u_high[...], u_rest[...] = split(u[k, j])
            for t in range(CORES):
                rows = pl.ds(t * half, half)
                acc[j, rows] -= live * product(low_high[k, rows], low_rest[k, rows], u_high[...], u_rest[...])

        if j < per_block:
            pl.when(pcol > k)(run)
        else:
            run()

    def store_lower(k):
        @pl.when(pcol == k)
        def _():
            for j in range(per_block):
                acc[j] = low[k, :, pl.ds(j * chunk, chunk)]

    for j in range(chunks):
        acc_load(j).start()

    @pl.when(first_chip & active)
    def _():
        for k in range(2):
            pivot_own(k).start()
        pltpu.make_async_copy(mat.at[own_rows(), pl.ds(0, width)], a.at[core], a_own).start()

    barrier = pltpu.get_barrier_semaphore()
    for other in range(n_row):
        @pl.when(z != other)
        def _():
            pl.semaphore_signal(barrier, inc=1, device_id=(other, pcol), device_id_type=MESH)
    for other in range(n_chip):
        @pl.when(chip != other)
        def _():
            pl.semaphore_signal(barrier, inc=1, device_id=(z, other * CORES + core), device_id_type=MESH)
    pl.semaphore_signal(barrier, inc=1, device_id=partner, device_id_type=MESH)
    pl.semaphore_wait(barrier, n_row + n_chip - 1)

    def swap_columns():
        source = mat.at[pl.ds(pl.multiple_of((1 - core) * half, 8), half), pl.ds(0, width)]
        return remote(source, a.at[core], a_send, a_recv, partner)

    def swapped_columns():
        return remote(a.at[1 - core], a.at[1 - core], a_send, a_recv, partner)

    @pl.when(first_chip)
    def _():
        for k in range(2):
            for target in range(n_row - 1, k, -1):
                @pl.when(z != target)
                def _():
                    pivot_send(k, target).start()

        @pl.when(active)
        def _():
            swap_columns().start()

    for j in range(chunks):
        acc_load(j).wait()

    @pl.when(z == 0)
    def _():
        originate(0, 0, steps)
        for j in range(chunks):
            out_store(j).start()

    @pl.when(active)
    def _():
        @pl.when(first_chip)
        def _():
            gather_pivot(0)
            pltpu.make_async_copy(mat.at[own_rows(), pl.ds(0, width)], a.at[core], a_own).wait()
            swapped_columns().wait_recv()
            apply_pivot(0, a[0])

        relay(0, 0, per_block * pieces)

        @pl.when(first_chip & both)
        def _():
            top = u.at[0, pl.ds(0, per_block)]
            copy = remote(top, top, t_send, t_recv, partner)

            @pl.when(core == 1)
            def _():
                copy.start()

            gather_pivot(1)

            @pl.when(core == 0)
            def _():
                copy.wait_recv()

            live = col_live[0, 1].astype(jnp.float32)
            left = split(low[0, own_rows()])
            for q in range(per_block):
                columns = pl.ds(q * chunk, chunk)
                a[1, :, columns] -= live * product(*left, *split(u[0, q]))
            apply_pivot(1, a[1])

            @pl.when(core == 1)
            def _():
                copy.wait_send()

        relay(0, per_block * pieces, steps - TAIL)
        take_lower(0)
        for j in range(chunks - 1):
            update(0, j)
            relay(0, steps - TAIL + j, steps - TAIL + j + 1)
        relay(0, steps - TAIL + chunks - 1, steps)

        @pl.when(z == 1)
        def _():
            @pl.when(z < last)
            def _():
                originate(1, 0, steps - pieces)

            update(0, chunks - 1)

            @pl.when(z < last)
            def _():
                originate(1, steps - pieces, steps)

            store_lower(0)
            for j in range(chunks):
                out_store(j).start()

        @pl.when(both)
        def _():
            relay(1, 0, pieces)
            update(0, chunks - 1)
            relay(1, pieces, steps - pieces)
            take_lower(1)
            for j in range(chunks - 1):
                update(1, j)
                if j == per_block - 1:
                    store_lower(0)
                    store_lower(1)
                    for done in range(per_block):
                        out_store(done).start()
                elif j >= per_block:
                    out_store(j).start()
                relay(1, steps - pieces + 2 * j, steps - pieces + 2 * j + 2)
            relay(1, steps - pieces + 2 * (chunks - 1), steps)
            update(1, chunks - 1)
            out_store(chunks - 1).start()

    @pl.when(z == 0)
    def _():
        finish_sends(0, origin_copy)

    @pl.when(active & (z < last))
    def _():
        finish_sends(0, relay_copy)

        @pl.when(z == 1)
        def _():
            finish_sends(1, origin_copy)

        @pl.when(both)
        def _():
            finish_sends(1, relay_copy)

    @pl.when(first_chip)
    def _():
        for k in range(2):
            for target in range(n_row - 1, k, -1):
                @pl.when(z != target)
                def _():
                    pivot_send(k, target).wait_send()

    @pl.when(first_chip & (z == 1))
    def _():
        pivot_own(1).wait()

    for k in range(2):
        @pl.when(z > k)
        def _():
            lower_pass(k).wait_send()

            @pl.when(first_chip)
            def _():
                for target in range(n_chip - 1, 0, -1):
                    lower_send(k, target).wait_send()
                for source in range(n_row):
                    @pl.when(z != source)
                    def _():
                        pivot_pass(k, source).wait_send()
                if k == 0:
                    swap_columns().wait_send()

    for j in range(chunks):
        out_store(j).wait()


def per_device(n_row, n_col, matrix, pivot_inverse, row_live, col_live):
    rows, columns = matrix.shape
    panels, rows_own, width = pivot_inverse.shape
    chunk = min(CHUNK, width)
    chunks = columns // chunk
    steps = chunks * PIECES
    f32, bf16, dma = jnp.float32, jnp.bfloat16, pltpu.SemaphoreType.DMA
    return pl.pallas_call(
        functools.partial(kernel, n_row, n_col),
        out_shape=jax.ShapeDtypeStruct((rows, columns), f32),
        in_specs=[pl.BlockSpec(memory_space=pltpu.SMEM)] * 2 + [pl.BlockSpec(memory_space=pl.ANY)] * 2,
        out_specs=pl.BlockSpec(memory_space=pl.ANY),
        scratch_shapes=[
            pltpu.VMEM((chunks, rows, chunk), f32),
            pltpu.VMEM((panels, chunks, width, chunk), f32),
            pltpu.VMEM((panels, width, width), f32),
            pltpu.VMEM((CORES, width // CORES, width), f32),
            pltpu.VMEM((panels, width, width), f32),
            pltpu.VMEM((panels, width, width), bf16),
            pltpu.VMEM((panels, width, width), bf16),
            pltpu.VMEM((width, chunk), bf16),
            pltpu.VMEM((width, chunk), bf16),
            dma((chunks,)), dma((chunks,)),
            dma((panels, steps)), dma((panels, steps)),
            dma((panels, n_row)), dma((panels, n_row)), dma((panels, n_row)), dma((panels, n_row)),
            dma((panels,)), dma, dma, dma, dma, dma,
            dma((panels, n_col // CORES)), dma((panels,)), dma((panels,)), dma((panels,)),
        ],
        compiler_params=pltpu.CompilerParams(
            collective_id=0, has_side_effects=True, vmem_limit_bytes=48 << 20
        ),
    )(row_live, col_live, matrix, pivot_inverse)


def solution(mesh):
    n_row, n_col = mesh.shape["prow"], mesh.shape["pcol"]
    return jax.shard_map(
        functools.partial(per_device, n_row, n_col),
        mesh=mesh,
        in_specs=(P("prow", "pcol"), P(None, "prow", None), P(), P()),
        out_specs=P("prow", "pcol"),
        check_vma=False,
    )
```

```python
import functools

import jax
import jax.numpy as jnp
from jax import lax
from jax.experimental import pallas as pl
from jax.experimental.pallas import tpu as pltpu
from jax.sharding import PartitionSpec as P

MESH = pl.DeviceIdType.MESH
CORES = 2
CHUNK = 256
PIECES = 16
TAIL = 4
GRANT = 67_043_328


def split(x):
    high = x.astype(jnp.bfloat16)
    return high, (x - high.astype(jnp.float32)).astype(jnp.bfloat16)


def product(left_high, left_low, right_high, right_low):
    dot = functools.partial(jnp.dot, preferred_element_type=jnp.float32)
    return dot(left_high, right_high) + (dot(left_high, right_low) + dot(left_low, right_high))


def kernel(
    n_row, n_col, chunk, row_hbm, col_hbm, mat, piv, acc,
    row_smem, col_smem, u, p, a, low, low_high, low_rest, u_high, u_rest,
    acc_sem, mask_sem, u_send, u_recv, p_send, p_recv, p_pass, p_passed, p_own,
    a_own, a_send, a_recv, t_send, t_recv, l_send, l_recv, l_pass, l_passed,
):
    z, pcol = lax.axis_index("prow"), lax.axis_index("pcol")
    core, chip = lax.rem(pcol, CORES), lax.div(pcol, CORES)
    n_chip = n_col // CORES
    partner = (z, pcol + 1 - 2 * core)
    width, half = piv.shape[2], piv.shape[2] // CORES
    rows_own = piv.shape[1]
    rows_half = rows_own // CORES
    chunks = acc.shape[1] // chunk
    per_block = width // chunk
    pieces = u_send.shape[1] // chunks
    piece = width // pieces
    steps = chunks * pieces
    last = n_row - 1
    first_chip, active, both = chip == 0, z > 0, z > 1

    def remote(src, dst, send, recv, to):
        return pltpu.make_async_remote_copy(
            src_ref=src, dst_ref=dst, send_sem=send, recv_sem=recv, device_id=to, device_id_type=MESH
        )

    load = pltpu.make_async_copy(mat, acc, acc_sem)
    masks = [
        pltpu.make_async_copy(row_hbm, row_smem, mask_sem.at[0]),
        pltpu.make_async_copy(col_hbm, col_smem, mask_sem.at[1]),
    ]

    def columns_of(j):
        start = j * chunk
        return pl.ds(start if isinstance(j, int) else pl.multiple_of(start, 128), chunk)

    def pivot_own(k):
        return pltpu.make_async_copy(piv.at[k], p.at[k, pl.ds(z * rows_own, rows_own)], p_own.at[k])

    def pivot_rows(k, source):
        return p.at[k, pl.ds(pl.multiple_of(source * rows_own + core * rows_half, 8), rows_half)]

    def pivot_send(k, target):
        return remote(
            piv.at[k, pl.ds(pl.multiple_of(core * rows_half, 8), rows_half)],
            pivot_rows(k, z), p_send.at[k, target], p_recv.at[k, z], (target, pcol),
        )

    def pivot_landed(k, source):
        return remote(pivot_rows(k, source), pivot_rows(k, source), p_send.at[k, source], p_recv.at[k, source], (z, pcol))

    def pivot_pass(k, source):
        return remote(pivot_rows(k, source), pivot_rows(k, source), p_pass.at[k, source], p_passed.at[k, source], partner)

    def piece_of(ref, j, r):
        return ref.at[j, pl.ds(pl.multiple_of(r * piece, 8), piece)]

    def relay_copy(k, s):
        place = piece_of(u.at[k], s // pieces, s % pieces)
        return remote(place, place, u_send.at[k, s], u_recv.at[k, s], (z + 1, pcol))

    def origin_copy(k, s):
        j, r = s // pieces, s % pieces
        rows = pl.ds(pl.multiple_of(r * piece, 8), piece)
        return remote(acc.at[rows, columns_of(j)], piece_of(u.at[k], j, r), u_send.at[k, s], u_recv.at[k, s], (z + 1, pcol))

    def start_of(k):
        return jnp.where(pcol <= k, per_block * pieces, 0)

    def relay(k, begin, end):
        def body(s, carry):
            copy = relay_copy(k, s)
            copy.wait_recv()

            @pl.when(z < last)
            def _():
                copy.start()

            return carry

        lax.fori_loop(jnp.maximum(begin, start_of(k)), end, body, 0)

    def originate(k, begin, end):
        def body(s, carry):
            origin_copy(k, s).start()
            return carry

        lax.fori_loop(jnp.maximum(begin, start_of(k)), end, body, 0)

    def finish_sends(k, copy):
        def body(s, carry):
            copy(k, s).wait_send()
            return carry

        lax.fori_loop(start_of(k), steps, body, 0)

    def own_rows():
        return pl.ds(pl.multiple_of(core * half, 8), half)

    def lower_send(k, target):
        rows = low.at[k, own_rows()]
        return remote(rows, rows, l_send.at[k, target], l_recv.at[k], (z, target * CORES + core))

    def lower_pass(k):
        rows = low.at[k, own_rows()]
        return remote(rows, rows, l_pass.at[k], l_passed.at[k], partner)

    def row_mask(k):
        return row_smem[k, z].astype(jnp.float32)

    def gather_pivot(k):
        for source in range(n_row):
            @pl.when(z != source)
            def _():
                pivot_landed(k, source).wait_recv()
                pivot_pass(k, source).start()
        pivot_own(k).wait()
        for source in range(n_row):
            @pl.when(z != source)
            def _():
                pivot_pass(k, source).wait_recv()

    def apply_pivot(k, left):
        left_high, left_low = split(left)
        for q in range(per_block):
            columns = pl.ds(q * chunk, chunk)
            right = split(p[k, :, columns])
            low[k, own_rows(), columns] = row_mask(k) * product(left_high, left_low, *right)
        for target in range(n_chip - 1, 0, -1):
            lower_send(k, target).start()
        lower_pass(k).start()

    def take_lower(k):
        @pl.when(chip > 0)
        def _():
            lower_send(k, 0).wait_recv()
            lower_pass(k).start()

        lower_pass(k).wait_recv()
        low_high[k], low_rest[k] = split(low[k])

    def update(k, j):
        live = col_smem[k, pcol + (j // per_block) * n_col].astype(jnp.float32)

        def run():
            u_high[...], u_rest[...] = split(u[k, j])
            for t in range(CORES):
                rows = pl.ds(t * half, half)
                acc[rows, columns_of(j)] -= live * product(low_high[k, rows], low_rest[k, rows], u_high[...], u_rest[...])

        if j < per_block:
            pl.when(pcol > k)(run)
        else:
            run()

    def store_lower(k):
        @pl.when(pcol == k)
        def _():
            acc[:, pl.ds(0, width)] = low[k]

    load.start()
    for copy in masks:
        copy.start()

    @pl.when(first_chip & active)
    def _():
        for k in range(2):
            pivot_own(k).start()
        pltpu.make_async_copy(mat.at[own_rows(), pl.ds(0, width)], a.at[core], a_own).start()

    barrier = pltpu.get_barrier_semaphore()
    for other in range(n_row):
        @pl.when(z != other)
        def _():
            pl.semaphore_signal(barrier, inc=1, device_id=(other, pcol), device_id_type=MESH)
    for other in range(n_chip):
        @pl.when(chip != other)
        def _():
            pl.semaphore_signal(barrier, inc=1, device_id=(z, other * CORES + core), device_id_type=MESH)
    pl.semaphore_signal(barrier, inc=1, device_id=partner, device_id_type=MESH)
    pl.semaphore_wait(barrier, n_row + n_chip - 1)

    def swap_columns():
        source = mat.at[pl.ds(pl.multiple_of((1 - core) * half, 8), half), pl.ds(0, width)]
        return remote(source, a.at[core], a_send, a_recv, partner)

    def swapped_columns():
        return remote(a.at[1 - core], a.at[1 - core], a_send, a_recv, partner)

    @pl.when(first_chip)
    def _():
        for k in range(2):
            for target in range(n_row - 1, k, -1):
                @pl.when(z != target)
                def _():
                    pivot_send(k, target).start()

        @pl.when(active)
        def _():
            swap_columns().start()

    for copy in masks:
        copy.wait()
    load.wait()

    @pl.when(z == 0)
    def _():
        originate(0, 0, steps)

    @pl.when(active)
    def _():
        @pl.when(first_chip)
        def _():
            gather_pivot(0)
            pltpu.make_async_copy(mat.at[own_rows(), pl.ds(0, width)], a.at[core], a_own).wait()
            swapped_columns().wait_recv()
            apply_pivot(0, a[0])

        relay(0, 0, per_block * pieces)

        @pl.when(first_chip & both)
        def _():
            top = u.at[0, pl.ds(0, per_block)]
            copy = remote(top, top, t_send, t_recv, partner)

            @pl.when(core == 1)
            def _():
                copy.start()

            gather_pivot(1)

            @pl.when(core == 0)
            def _():
                copy.wait_recv()

            live = col_smem[0, 1].astype(jnp.float32)
            left = split(low[0, own_rows()])
            for q in range(per_block):
                columns = pl.ds(q * chunk, chunk)
                a[1, :, columns] -= live * product(*left, *split(u[0, q]))
            apply_pivot(1, a[1])

            @pl.when(core == 1)
            def _():
                copy.wait_send()

        relay(0, per_block * pieces, steps - TAIL)
        take_lower(0)
        for j in range(chunks - 1):
            update(0, j)
            relay(0, steps - TAIL + j, steps - TAIL + j + 1)
        relay(0, steps - TAIL + chunks - 1, steps)

        @pl.when(z == 1)
        def _():
            @pl.when(z < last)
            def _():
                originate(1, 0, steps - pieces)

            update(0, chunks - 1)

            @pl.when(z < last)
            def _():
                originate(1, steps - pieces, steps)

            store_lower(0)

        @pl.when(both)
        def _():
            relay(1, 0, pieces)
            update(0, chunks - 1)
            relay(1, pieces, steps - pieces)
            take_lower(1)
            for j in range(chunks - 1):
                update(1, j)
                if j == per_block - 1:
                    store_lower(0)
                    store_lower(1)
                relay(1, steps - pieces + 4 * j, steps - pieces + 4 * j + 4)
            relay(1, steps - pieces + 4 * (chunks - 1), steps)
            update(1, chunks - 1)

    @pl.when(z == 0)
    def _():
        finish_sends(0, origin_copy)

    @pl.when(active & (z < last))
    def _():
        finish_sends(0, relay_copy)

        @pl.when(z == 1)
        def _():
            finish_sends(1, origin_copy)

        @pl.when(both)
        def _():
            finish_sends(1, relay_copy)

    @pl.when(first_chip)
    def _():
        for k in range(2):
            for target in range(n_row - 1, k, -1):
                @pl.when(z != target)
                def _():
                    pivot_send(k, target).wait_send()

    @pl.when(first_chip & (z == 1))
    def _():
        pivot_own(1).wait()

    for k in range(2):
        @pl.when(z > k)
        def _():
            lower_pass(k).wait_send()

            @pl.when(first_chip)
            def _():
                for target in range(n_chip - 1, 0, -1):
                    lower_send(k, target).wait_send()
                for source in range(n_row):
                    @pl.when(z != source)
                    def _():
                        pivot_pass(k, source).wait_send()
                if k == 0:
                    swap_columns().wait_send()


def per_device(n_row, n_col, matrix, pivot_inverse, row_live, col_live):
    rows, columns = matrix.shape
    panels, rows_own, width = pivot_inverse.shape
    chunk = min(CHUNK, width)
    chunks = columns // chunk
    steps = chunks * PIECES
    f32, bf16, dma = jnp.float32, jnp.bfloat16, pltpu.SemaphoreType.DMA
    return pl.pallas_call(
        functools.partial(kernel, n_row, n_col, chunk),
        out_shape=pltpu.VMEM((rows, columns), f32),
        in_specs=[pl.BlockSpec(memory_space=pltpu.HBM)] * 4,
        out_specs=pl.BlockSpec(memory_space=pltpu.VMEM),
        scratch_shapes=[
            pltpu.SMEM(row_live.shape, jnp.int32),
            pltpu.SMEM(col_live.shape, jnp.int32),
            pltpu.VMEM((panels, chunks, width, chunk), f32),
            pltpu.VMEM((panels, width, width), f32),
            pltpu.VMEM((CORES, width // CORES, width), f32),
            pltpu.VMEM((panels, width, width), f32),
            pltpu.VMEM((panels, width, width), bf16),
            pltpu.VMEM((panels, width, width), bf16),
            pltpu.VMEM((width, chunk), bf16),
            pltpu.VMEM((width, chunk), bf16),
            dma, dma((2,)),
            dma((panels, steps)), dma((panels, steps)),
            dma((panels, n_row)), dma((panels, n_row)), dma((panels, n_row)), dma((panels, n_row)),
            dma((panels,)), dma, dma, dma, dma, dma,
            dma((panels, n_col // CORES)), dma((panels,)), dma((panels,)), dma((panels,)),
        ],
        compiler_params=pltpu.CompilerParams(
            collective_id=0, has_side_effects=True, vmem_limit_bytes=GRANT - 4 * rows * columns
        ),
    )(row_live, col_live, matrix, pivot_inverse)


def solution(mesh):
    n_row, n_col = mesh.shape["prow"], mesh.shape["pcol"]
    return jax.shard_map(
        functools.partial(per_device, n_row, n_col),
        mesh=mesh,
        in_specs=(P("prow", "pcol"), P(None, "prow", None), P(), P()),
        out_specs=P("prow", "pcol"),
        check_vma=False,
    )
```

```python
import functools

import jax
import jax.numpy as jnp
from jax import lax
from jax.experimental import pallas as pl
from jax.experimental.pallas import tpu as pltpu
from jax.sharding import PartitionSpec as P

MESH = pl.DeviceIdType.MESH
CORES = 2
CHUNK = 256
PIECES = 16
TAIL = 4
GUESTS = 24
GRANT = 67_043_328


def split(x):
    high = x.astype(jnp.bfloat16)
    return high, (x - high.astype(jnp.float32)).astype(jnp.bfloat16)


def product(left_high, left_low, right_high, right_low):
    dot = functools.partial(jnp.dot, preferred_element_type=jnp.float32)
    return dot(left_high, right_high) + (dot(left_high, right_low) + dot(left_low, right_high))


def kernel(
    n_row, n_col, chunk, row_hbm, col_hbm, mat, piv, acc,
    row_smem, col_smem, u, p, a, guest, low, low_high, low_rest, u_high, u_rest,
    acc_sem, mask_sem, u_send, u_recv, p_send, p_recv, p_pass, p_passed, p_own,
    a_own, a_send, a_recv, t_send, t_recv, l_send, l_recv, l_pass, l_passed,
    p_up, g_in, g_recv, g_down, g_out,
):
    z, pcol = lax.axis_index("prow"), lax.axis_index("pcol")
    core, chip = lax.rem(pcol, CORES), lax.div(pcol, CORES)
    n_chip = n_col // CORES
    partner = (z, pcol + 1 - 2 * core)
    width, half = piv.shape[2], piv.shape[2] // CORES
    rows_own = piv.shape[1]
    rows_half = rows_own // CORES
    chunks = acc.shape[1] // chunk
    per_block = width // chunk
    pieces = u_send.shape[1] // chunks
    piece = width // pieces
    steps = chunks * pieces
    last = n_row - 1
    guests = guest.shape[1]
    guest_start = (chunks - 2) * pieces
    first_chip, active, both = chip == 0, z > 0, z > 1
    guest_end = guest_start + jnp.where(chip > 0, guests, 0)

    def remote(src, dst, send, recv, to):
        return pltpu.make_async_remote_copy(
            src_ref=src, dst_ref=dst, send_sem=send, recv_sem=recv, device_id=to, device_id_type=MESH
        )

    load = pltpu.make_async_copy(mat, acc, acc_sem)
    masks = [
        pltpu.make_async_copy(row_hbm, row_smem, mask_sem.at[0]),
        pltpu.make_async_copy(col_hbm, col_smem, mask_sem.at[1]),
    ]

    def columns_of(j):
        start = j * chunk
        return pl.ds(start if isinstance(j, int) else pl.multiple_of(start, 128), chunk)

    def pivot_own(k):
        return pltpu.make_async_copy(piv.at[k], p.at[k, pl.ds(z * rows_own, rows_own)], p_own.at[k])

    def pivot_rows(k, source):
        return p.at[k, pl.ds(pl.multiple_of(source * rows_own + core * rows_half, 8), rows_half)]

    def pivot_send(k, target, send):
        return remote(
            piv.at[k, pl.ds(pl.multiple_of(core * rows_half, 8), rows_half)],
            pivot_rows(k, z), send, p_recv.at[k, z], (target, pcol),
        )

    def pivot_relay(k, source, target):
        return remote(pivot_rows(k, source), pivot_rows(k, source), p_send.at[k, source], p_recv.at[k, source], (target, pcol))

    def pivot_landed(k, source):
        return remote(pivot_rows(k, source), pivot_rows(k, source), p_send.at[k, source], p_recv.at[k, source], (z, pcol))

    def pivot_pass(k, source):
        return remote(pivot_rows(k, source), pivot_rows(k, source), p_pass.at[k, source], p_passed.at[k, source], partner)

    def piece_of(ref, j, r):
        return ref.at[j, pl.ds(pl.multiple_of(r * piece, 8), piece)]

    def relay_copy(k, s):
        place = piece_of(u.at[k], s // pieces, s % pieces)
        return remote(place, place, u_send.at[k, s], u_recv.at[k, s], (z + 1, pcol))

    def origin_copy(k, s):
        j, r = s // pieces, s % pieces
        rows = pl.ds(pl.multiple_of(r * piece, 8), piece)
        return remote((acc if k else mat).at[rows, columns_of(j)], piece_of(u.at[k], j, r), u_send.at[k, s], u_recv.at[k, s], (z + 1, pcol))

    def start_of(k):
        return jnp.where(pcol <= k, per_block * pieces, 0)

    def relay(k, begin, end):
        def body(s, carry):
            copy = relay_copy(k, s)
            copy.wait_recv()

            @pl.when(z < last)
            def _():
                copy.start()

            return carry

        lax.fori_loop(jnp.maximum(begin, start_of(k)), end, body, 0)

    def originate(k, begin, end):
        def body(s, carry):
            origin_copy(k, s).start()
            return carry

        lax.fori_loop(jnp.maximum(begin, start_of(k)), end, body, 0)

    def finish_sends(k, copy):
        def body(s, carry):
            copy(k, s).wait_send()
            return carry

        if k:
            lax.fori_loop(start_of(k), guest_start, body, 0)
            lax.fori_loop(guest_end, steps, body, 0)
        else:
            lax.fori_loop(start_of(k), steps, body, 0)

    def guest_in(i):
        rows = pl.ds(i * piece, piece)
        source = acc.at[rows, columns_of(guest_start // pieces)]
        return remote(source, guest.at[chip, i], g_in.at[i], g_recv.at[chip, i], (z, core))

    def guest_down(q, i):
        return remote(guest.at[q, i], guest.at[q, i], g_down.at[q, i], g_recv.at[q, i], (z + 1, pcol))

    def guest_out(q, i):
        target = piece_of(u.at[1], guest_start // pieces, i)
        return remote(guest.at[q, i], target, g_out.at[q, i], u_recv.at[1, guest_start + i], (z, q * CORES + core))

    def pass_guests():
        def body(t, carry):
            q, i = 1 + t // guests, t % guests
            guest_down(q, i).wait_recv()

            @pl.when(z < last)
            def _():
                guest_down(q, i).start()

            @pl.when(both)
            def _():
                guest_out(q, i).start()

            return carry

        lax.fori_loop(0, (n_chip - 1) * guests, body, 0)

    def finish_guests():
        def body(t, carry):
            q, i = 1 + t // guests, t % guests

            @pl.when(z < last)
            def _():
                guest_down(q, i).wait_send()

            @pl.when(both)
            def _():
                guest_out(q, i).wait_send()

            return carry

        lax.fori_loop(0, (n_chip - 1) * guests, body, 0)

    def own_rows():
        return pl.ds(pl.multiple_of(core * half, 8), half)

    def lower_send(k, target):
        rows = low.at[k, own_rows()]
        return remote(rows, rows, l_send.at[k, target], l_recv.at[k], (z, target * CORES + core))

    def lower_pass(k):
        rows = low.at[k, own_rows()]
        return remote(rows, rows, l_pass.at[k], l_passed.at[k], partner)

    def row_mask(k):
        return row_smem[k, z].astype(jnp.float32)

    def for_sources(k, visit):
        for distance in range(1, n_row):
            @pl.when(z - distance >= 0)
            def _():
                visit(z - distance, z + 1, z < last, z > k)

            @pl.when((z + distance <= last) & (z > k))
            def _():
                visit(z + distance, z - 1, z - 1 > k, z > k)

    def relay_pivot(k):
        def visit(source, target, onward, used):
            pivot_landed(k, source).wait_recv()

            @pl.when(onward)
            def _():
                pivot_relay(k, source, target).start()

            @pl.when(used)
            def _():
                pivot_pass(k, source).start()

        for_sources(k, visit)

    def gather_pivot(k):
        pivot_own(k).wait()
        for source in range(n_row):
            @pl.when(z != source)
            def _():
                pivot_pass(k, source).wait_recv()

    def finish_pivot(k):
        def visit(source, target, onward, used):
            @pl.when(onward)
            def _():
                pivot_relay(k, source, target).wait_send()

            @pl.when(used)
            def _():
                pivot_pass(k, source).wait_send()

        for_sources(k, visit)

    def apply_pivot(k, left):
        left_high, left_low = split(left)
        for q in range(per_block):
            columns = pl.ds(q * chunk, chunk)
            right = split(p[k, :, columns])
            low[k, own_rows(), columns] = row_mask(k) * product(left_high, left_low, *right)
        for target in range(n_chip - 1, 0, -1):
            lower_send(k, target).start()
        lower_pass(k).start()

    def take_lower(k):
        @pl.when(chip > 0)
        def _():
            lower_send(k, 0).wait_recv()
            lower_pass(k).start()

        lower_pass(k).wait_recv()
        low_high[k], low_rest[k] = split(low[k])

    def update(k, j, part=0, parts=1):
        live = col_smem[k, pcol + (j // per_block) * n_col].astype(jnp.float32)

        def run():
            depth = pl.ds(part * (width // parts), width // parts)
            u_high[depth], u_rest[depth] = split(u[k, j, depth])
            for t in range(CORES):
                rows = pl.ds(t * half, half)
                left = low_high[k, rows, depth], low_rest[k, rows, depth]
                acc[rows, columns_of(j)] -= live * product(*left, u_high[depth], u_rest[depth])

        if j < per_block:
            pl.when(pcol > k)(run)
        else:
            run()

    def store_lower(k):
        @pl.when(pcol == k)
        def _():
            acc[:, pl.ds(0, width)] = low[k]

    load.start()
    for copy in masks:
        copy.start()

    @pl.when(first_chip & active)
    def _():
        for k in range(2):
            pivot_own(k).start()
        pltpu.make_async_copy(mat.at[own_rows(), pl.ds(0, width)], a.at[core], a_own).start()

    barrier = pltpu.get_barrier_semaphore()
    for other in range(n_row):
        @pl.when(z != other)
        def _():
            pl.semaphore_signal(barrier, inc=1, device_id=(other, pcol), device_id_type=MESH)
    for other in range(n_chip):
        @pl.when(chip != other)
        def _():
            pl.semaphore_signal(barrier, inc=1, device_id=(z, other * CORES + core), device_id_type=MESH)
    pl.semaphore_signal(barrier, inc=1, device_id=partner, device_id_type=MESH)
    pl.semaphore_wait(barrier, n_row + n_chip - 1)

    def swap_columns():
        source = mat.at[pl.ds(pl.multiple_of((1 - core) * half, 8), half), pl.ds(0, width)]
        return remote(source, a.at[core], a_send, a_recv, partner)

    def swapped_columns():
        return remote(a.at[1 - core], a.at[1 - core], a_send, a_recv, partner)

    @pl.when(first_chip)
    def _():
        for k in range(2):
            @pl.when(z < last)
            def _():
                pivot_send(k, z + 1, p_send.at[k, z]).start()

            @pl.when(z - 1 > k)
            def _():
                pivot_send(k, z - 1, p_up.at[k]).start()

        @pl.when(active)
        def _():
            swap_columns().start()

    @pl.when(z == 0)
    def _():
        originate(0, 0, steps)

    for copy in masks:
        copy.wait()
    load.wait()

    @pl.when(active)
    def _():
        @pl.when(first_chip)
        def _():
            relay_pivot(0)
            gather_pivot(0)
            pltpu.make_async_copy(mat.at[own_rows(), pl.ds(0, width)], a.at[core], a_own).wait()
            swapped_columns().wait_recv()
            apply_pivot(0, a[0])
            relay_pivot(1)

        relay(0, 0, per_block * pieces)

        @pl.when(first_chip & both)
        def _():
            top = u.at[0, pl.ds(0, per_block)]
            copy = remote(top, top, t_send, t_recv, partner)

            @pl.when(core == 1)
            def _():
                copy.start()

            gather_pivot(1)

            @pl.when(core == 0)
            def _():
                copy.wait_recv()

            live = col_smem[0, 1].astype(jnp.float32)
            left = split(low[0, own_rows()])
            for q in range(per_block):
                columns = pl.ds(q * chunk, chunk)
                a[1, :, columns] -= live * product(*left, *split(u[0, q]))
            apply_pivot(1, a[1])

            @pl.when(core == 1)
            def _():
                copy.wait_send()

        relay(0, per_block * pieces, steps - TAIL)
        take_lower(0)
        for j in range(chunks - 1):
            update(0, j)
            relay(0, steps - TAIL + j, steps - TAIL + j + 1)
        relay(0, steps - TAIL + chunks - 1, steps)

        @pl.when(z == 1)
        def _():
            @pl.when(z < last)
            def _():
                @pl.when(chip > 0)
                def _():
                    for i in range(guests):
                        guest_in(i).start()

                originate(1, 0, guest_start)
                originate(1, guest_end, steps - pieces)

                @pl.when(first_chip)
                def _():
                    pass_guests()

            update(0, chunks - 1)

            @pl.when(z < last)
            def _():
                originate(1, steps - pieces, steps)

            store_lower(0)

        @pl.when(both)
        def _():
            relay(1, 0, pieces)
            update(0, chunks - 1)
            relay(1, pieces, guest_start)
            take_lower(1)
            update(1, 0)
            relay(1, guest_end, guest_end + 4)
            update(1, 1)
            store_lower(0)
            store_lower(1)
            relay(1, guest_end + 4, steps - pieces)

            @pl.when(first_chip)
            def _():
                pass_guests()

            @pl.when(chip > 0)
            def _():
                for i in range(guests):
                    relay_copy(1, guest_start + i).wait_recv()

            for j in range(2, chunks - 1):
                update(1, j)
            for part in range(4):
                begin = steps - pieces + part * (pieces // 4)
                relay(1, begin, begin + pieces // 4)
                update(1, chunks - 1, part, 4)

    @pl.when(z == 0)
    def _():
        finish_sends(0, origin_copy)

    @pl.when(active & first_chip)
    def _():
        @pl.when((z < last) | both)
        def _():
            finish_guests()

    @pl.when((z == 1) & (z < last) & (chip > 0))
    def _():
        for i in range(guests):
            guest_in(i).wait_send()

    @pl.when(active & (z < last))
    def _():
        finish_sends(0, relay_copy)

        @pl.when(z == 1)
        def _():
            finish_sends(1, origin_copy)

        @pl.when(both)
        def _():
            finish_sends(1, relay_copy)

    @pl.when(first_chip)
    def _():
        for k in range(2):
            @pl.when(z < last)
            def _():
                pivot_send(k, z + 1, p_send.at[k, z]).wait_send()

            @pl.when(z - 1 > k)
            def _():
                pivot_send(k, z - 1, p_up.at[k]).wait_send()

            finish_pivot(k)

    @pl.when(first_chip & (z == 1))
    def _():
        pivot_own(1).wait()

    for k in range(2):
        @pl.when(z > k)
        def _():
            lower_pass(k).wait_send()

            @pl.when(first_chip)
            def _():
                for target in range(n_chip - 1, 0, -1):
                    lower_send(k, target).wait_send()
                if k == 0:
                    swap_columns().wait_send()


def per_device(n_row, n_col, matrix, pivot_inverse, row_live, col_live):
    rows, columns = matrix.shape
    panels, rows_own, width = pivot_inverse.shape
    chunk = min(CHUNK, width)
    chunks = columns // chunk
    steps = chunks * PIECES
    n_chip = n_col // CORES
    guests = max(1, GUESTS // n_chip)
    f32, bf16, dma = jnp.float32, jnp.bfloat16, pltpu.SemaphoreType.DMA
    return pl.pallas_call(
        functools.partial(kernel, n_row, n_col, chunk),
        out_shape=pltpu.VMEM((rows, columns), f32),
        in_specs=[pl.BlockSpec(memory_space=pltpu.HBM)] * 4,
        out_specs=pl.BlockSpec(memory_space=pltpu.VMEM),
        scratch_shapes=[
            pltpu.SMEM(row_live.shape, jnp.int32),
            pltpu.SMEM(col_live.shape, jnp.int32),
            pltpu.VMEM((panels, chunks, width, chunk), f32),
            pltpu.VMEM((panels, width, width), f32),
            pltpu.VMEM((CORES, width // CORES, width), f32),
            pltpu.VMEM((n_chip, guests, width // PIECES, chunk), f32),
            pltpu.VMEM((panels, width, width), f32),
            pltpu.VMEM((panels, width, width), bf16),
            pltpu.VMEM((panels, width, width), bf16),
            pltpu.VMEM((width, chunk), bf16),
            pltpu.VMEM((width, chunk), bf16),
            dma, dma((2,)),
            dma((panels, steps)), dma((panels, steps)),
            dma((panels, n_row)), dma((panels, n_row)), dma((panels, n_row)), dma((panels, n_row)),
            dma((panels,)), dma, dma, dma, dma, dma,
            dma((panels, n_col // CORES)), dma((panels,)), dma((panels,)), dma((panels,)),
            dma((panels,)), dma((guests,)), dma((n_chip, guests)), dma((n_chip, guests)), dma((n_chip, guests)),
        ],
        compiler_params=pltpu.CompilerParams(
            collective_id=0, has_side_effects=True, vmem_limit_bytes=GRANT - 4 * rows * columns
        ),
    )(row_live, col_live, matrix, pivot_inverse)


def solution(mesh):
    n_row, n_col = mesh.shape["prow"], mesh.shape["pcol"]
    return jax.shard_map(
        functools.partial(per_device, n_row, n_col),
        mesh=mesh,
        in_specs=(P("prow", "pcol"), P(None, "prow", None), P(), P()),
        out_specs=P("prow", "pcol"),
        check_vma=False,
    )
```

```python
import functools

import jax
import jax.numpy as jnp
from jax import lax
from jax.experimental import pallas as pl
from jax.experimental.pallas import tpu as pltpu
from jax.sharding import PartitionSpec as P

MESH = pl.DeviceIdType.MESH
CORES = 2
CHUNK = 256
PIECES = 16
TAIL = 4
GUESTS = 24
GRANT = 67_043_328


def split(x):
    high = x.astype(jnp.bfloat16)
    return high, (x - high.astype(jnp.float32)).astype(jnp.bfloat16)


def product(left_high, left_low, right_high, right_low):
    dot = functools.partial(jnp.dot, preferred_element_type=jnp.float32)
    return dot(left_high, right_high) + (dot(left_high, right_low) + dot(left_low, right_high))


def kernel(
    n_row, n_col, chunk, row_hbm, col_hbm, mat, piv, acc,
    row_smem, col_smem, u, p, a, guest, low, low_high, low_rest, u_high, u_rest,
    acc_sem, mask_sem, u_send, u_recv, p_send, p_recv, p_pass, p_passed, p_own,
    a_own, a_send, a_recv, t_send, t_recv, l_send, l_recv, l_pass, l_passed,
    p_up, g_in, g_recv, g_down, g_out,
):
    z, pcol = lax.axis_index("prow"), lax.axis_index("pcol")
    core, chip = lax.rem(pcol, CORES), lax.div(pcol, CORES)
    n_chip = n_col // CORES
    partner = (z, pcol + 1 - 2 * core)
    width, half = piv.shape[2], piv.shape[2] // CORES
    rows_own = piv.shape[1]
    rows_half = rows_own // CORES
    chunks = acc.shape[1] // chunk
    per_block = width // chunk
    pieces = u_send.shape[1] // chunks
    piece = width // pieces
    steps = chunks * pieces
    last = n_row - 1
    guests = guest.shape[1]
    guest_start = (chunks - 2) * pieces
    first_chip, active, both = chip == 0, z > 0, z > 1
    guest_end = guest_start + jnp.where(chip > 0, guests, 0)

    def remote(src, dst, send, recv, to):
        return pltpu.make_async_remote_copy(
            src_ref=src, dst_ref=dst, send_sem=send, recv_sem=recv, device_id=to, device_id_type=MESH
        )

    load = pltpu.make_async_copy(mat, acc, acc_sem)
    masks = [
        pltpu.make_async_copy(row_hbm, row_smem, mask_sem.at[0]),
        pltpu.make_async_copy(col_hbm, col_smem, mask_sem.at[1]),
    ]

    def columns_of(j):
        start = j * chunk
        return pl.ds(start if isinstance(j, int) else pl.multiple_of(start, 128), chunk)

    def pivot_own(k):
        return pltpu.make_async_copy(piv.at[k], p.at[k, pl.ds(z * rows_own, rows_own)], p_own.at[k])

    def pivot_rows(k, source):
        return p.at[k, pl.ds(pl.multiple_of(source * rows_own + core * rows_half, 8), rows_half)]

    def pivot_send(k, target, send):
        return remote(
            piv.at[k, pl.ds(pl.multiple_of(core * rows_half, 8), rows_half)],
            pivot_rows(k, z), send, p_recv.at[k, z], (target, pcol),
        )

    def pivot_relay(k, source, target):
        return remote(pivot_rows(k, source), pivot_rows(k, source), p_send.at[k, source], p_recv.at[k, source], (target, pcol))

    def pivot_landed(k, source):
        return remote(pivot_rows(k, source), pivot_rows(k, source), p_send.at[k, source], p_recv.at[k, source], (z, pcol))

    def pivot_pass(k, source):
        return remote(pivot_rows(k, source), pivot_rows(k, source), p_pass.at[k, source], p_passed.at[k, source], partner)

    def piece_of(ref, j, r):
        return ref.at[j, pl.ds(pl.multiple_of(r * piece, 8), piece)]

    def relay_copy(k, s):
        place = piece_of(u.at[k], s // pieces, s % pieces)
        return remote(place, place, u_send.at[k, s], u_recv.at[k, s], (z + 1, pcol))

    def origin_copy(k, s):
        j, r = s // pieces, s % pieces
        rows = pl.ds(pl.multiple_of(r * piece, 8), piece)
        return remote(acc.at[rows, columns_of(j)], piece_of(u.at[k], j, r), u_send.at[k, s], u_recv.at[k, s], (z + 1, pcol))

    def start_of(k):
        return jnp.where(pcol <= k, per_block * pieces, 0)

    def relay(k, begin, end):
        def body(s, carry):
            copy = relay_copy(k, s)
            copy.wait_recv()

            @pl.when(z < last)
            def _():
                copy.start()

            return carry

        lax.fori_loop(jnp.maximum(begin, start_of(k)), end, body, 0)

    def originate(k, begin, end):
        def body(s, carry):
            origin_copy(k, s).start()
            return carry

        lax.fori_loop(jnp.maximum(begin, start_of(k)), end, body, 0)

    def finish_sends(k, copy):
        def body(s, carry):
            copy(k, s).wait_send()
            return carry

        if k:
            lax.fori_loop(start_of(k), guest_start, body, 0)
            lax.fori_loop(guest_end, steps, body, 0)
        else:
            lax.fori_loop(start_of(k), steps, body, 0)

    def guest_in(i):
        rows = pl.ds(i * piece, piece)
        source = acc.at[rows, columns_of(guest_start // pieces)]
        return remote(source, guest.at[chip, i], g_in.at[i], g_recv.at[chip, i], (z, core))

    def guest_down(q, i):
        return remote(guest.at[q, i], guest.at[q, i], g_down.at[q, i], g_recv.at[q, i], (z + 1, pcol))

    def guest_out(q, i):
        target = piece_of(u.at[1], guest_start // pieces, i)
        return remote(guest.at[q, i], target, g_out.at[q, i], u_recv.at[1, guest_start + i], (z, q * CORES + core))

    def pass_guests():
        def body(t, carry):
            q, i = 1 + t // guests, t % guests
            guest_down(q, i).wait_recv()

            @pl.when(z < last)
            def _():
                guest_down(q, i).start()

            @pl.when(both)
            def _():
                guest_out(q, i).start()

            return carry

        lax.fori_loop(0, (n_chip - 1) * guests, body, 0)

    def finish_guests():
        def body(t, carry):
            q, i = 1 + t // guests, t % guests

            @pl.when(z < last)
            def _():
                guest_down(q, i).wait_send()

            @pl.when(both)
            def _():
                guest_out(q, i).wait_send()

            return carry

        lax.fori_loop(0, (n_chip - 1) * guests, body, 0)

    def own_rows():
        return pl.ds(pl.multiple_of(core * half, 8), half)

    def lower_send(k, target):
        rows = low.at[k, own_rows()]
        return remote(rows, rows, l_send.at[k, target], l_recv.at[k], (z, target * CORES + core))

    def lower_pass(k):
        rows = low.at[k, own_rows()]
        return remote(rows, rows, l_pass.at[k], l_passed.at[k], partner)

    def row_mask(k):
        return row_smem[k, z].astype(jnp.float32)

    def for_sources(k, visit):
        for distance in range(1, n_row):
            @pl.when(z - distance >= 0)
            def _():
                visit(z - distance, z + 1, z < last, z > k)

            @pl.when((z + distance <= last) & (z > k))
            def _():
                visit(z + distance, z - 1, z - 1 > k, z > k)

    def relay_pivot(k):
        def visit(source, target, onward, used):
            pivot_landed(k, source).wait_recv()

            @pl.when(onward)
            def _():
                pivot_relay(k, source, target).start()

            @pl.when(used)
            def _():
                pivot_pass(k, source).start()

        for_sources(k, visit)

    def gather_pivot(k):
        pivot_own(k).wait()
        for source in range(n_row):
            @pl.when(z != source)
            def _():
                pivot_pass(k, source).wait_recv()

    def finish_pivot(k):
        def visit(source, target, onward, used):
            @pl.when(onward)
            def _():
                pivot_relay(k, source, target).wait_send()

            @pl.when(used)
            def _():
                pivot_pass(k, source).wait_send()

        for_sources(k, visit)

    def apply_pivot(k, left):
        left_high, left_low = split(left)
        for q in range(per_block):
            columns = pl.ds(q * chunk, chunk)
            right = split(p[k, :, columns])
            low[k, own_rows(), columns] = row_mask(k) * product(left_high, left_low, *right)
        for target in range(n_chip - 1, 0, -1):
            lower_send(k, target).start()
        lower_pass(k).start()

    def take_lower(k):
        @pl.when(chip > 0)
        def _():
            lower_send(k, 0).wait_recv()
            lower_pass(k).start()

        lower_pass(k).wait_recv()
        low_high[k], low_rest[k] = split(low[k])

    def update(k, j, part=0, parts=1):
        live = col_smem[k, pcol + (j // per_block) * n_col].astype(jnp.float32)

        def run():
            depth = pl.ds(part * (width // parts), width // parts)
            u_high[depth], u_rest[depth] = split(u[k, j, depth])
            for t in range(CORES):
                rows = pl.ds(t * half, half)
                left = low_high[k, rows, depth], low_rest[k, rows, depth]
                acc[rows, columns_of(j)] -= live * product(*left, u_high[depth], u_rest[depth])

        if j < per_block:
            pl.when(pcol > k)(run)
        else:
            run()

    def store_lower(k):
        @pl.when(pcol == k)
        def _():
            acc[:, pl.ds(0, width)] = low[k]

    load.start()
    for copy in masks:
        copy.start()

    @pl.when(first_chip & active)
    def _():
        for k in range(2):
            pivot_own(k).start()
        pltpu.make_async_copy(mat.at[own_rows(), pl.ds(0, width)], a.at[core], a_own).start()

    barrier = pltpu.get_barrier_semaphore()
    for other in range(n_row):
        @pl.when(z != other)
        def _():
            pl.semaphore_signal(barrier, inc=1, device_id=(other, pcol), device_id_type=MESH)
    for other in range(n_chip):
        @pl.when(chip != other)
        def _():
            pl.semaphore_signal(barrier, inc=1, device_id=(z, other * CORES + core), device_id_type=MESH)
    pl.semaphore_signal(barrier, inc=1, device_id=partner, device_id_type=MESH)
    pl.semaphore_wait(barrier, n_row + n_chip - 1)

    def swap_columns():
        source = mat.at[pl.ds(pl.multiple_of((1 - core) * half, 8), half), pl.ds(0, width)]
        return remote(source, a.at[core], a_send, a_recv, partner)

    def swapped_columns():
        return remote(a.at[1 - core], a.at[1 - core], a_send, a_recv, partner)

    @pl.when(first_chip)
    def _():
        for k in range(2):
            @pl.when(z < last)
            def _():
                pivot_send(k, z + 1, p_send.at[k, z]).start()

            @pl.when(z - 1 > k)
            def _():
                pivot_send(k, z - 1, p_up.at[k]).start()

        @pl.when(active)
        def _():
            swap_columns().start()

    load.wait()

    @pl.when(z == 0)
    def _():
        originate(0, 0, steps)

    for copy in masks:
        copy.wait()

    @pl.when(active)
    def _():
        @pl.when(first_chip)
        def _():
            relay_pivot(0)
            gather_pivot(0)
            pltpu.make_async_copy(mat.at[own_rows(), pl.ds(0, width)], a.at[core], a_own).wait()
            swapped_columns().wait_recv()
            apply_pivot(0, a[0])
            relay_pivot(1)

        ahead = jnp.where(pcol == 0, steps - TAIL, per_block * pieces)
        relay(0, 0, ahead)

        @pl.when(first_chip & both)
        def _():
            top = u.at[0, pl.ds(0, per_block)]
            copy = remote(top, top, t_send, t_recv, partner)

            @pl.when(core == 1)
            def _():
                copy.start()

            gather_pivot(1)

            @pl.when(core == 0)
            def _():
                copy.wait_recv()

            live = col_smem[0, 1].astype(jnp.float32)
            left = split(low[0, own_rows()])
            for q in range(per_block):
                columns = pl.ds(q * chunk, chunk)
                a[1, :, columns] -= live * product(*left, *split(u[0, q]))
            apply_pivot(1, a[1])

            @pl.when(core == 1)
            def _():
                copy.wait_send()

        relay(0, ahead, steps - TAIL)
        take_lower(0)
        for j in range(chunks - 1):
            update(0, j)
            relay(0, steps - TAIL + j, steps - TAIL + j + 1)
        relay(0, steps - TAIL + chunks - 1, steps)

        @pl.when(z == 1)
        def _():
            @pl.when(z < last)
            def _():
                @pl.when(chip > 0)
                def _():
                    for i in range(guests):
                        guest_in(i).start()

                originate(1, 0, guest_start)
                originate(1, guest_end, steps - pieces)

                @pl.when(first_chip)
                def _():
                    pass_guests()

            update(0, chunks - 1)

            @pl.when(z < last)
            def _():
                originate(1, steps - pieces, steps)

            store_lower(0)

        @pl.when(both)
        def _():
            relay(1, 0, pieces)
            update(0, chunks - 1)
            relay(1, pieces, guest_start)
            take_lower(1)
            update(1, 0)
            relay(1, guest_end, guest_end + 4)
            update(1, 1)
            store_lower(0)
            store_lower(1)
            relay(1, guest_end + 4, steps - pieces)

            @pl.when(first_chip)
            def _():
                pass_guests()

            @pl.when(chip > 0)
            def _():
                for i in range(guests):
                    relay_copy(1, guest_start + i).wait_recv()

            for j in range(2, chunks - 1):
                update(1, j)
            for part in range(4):
                begin = steps - pieces + part * (pieces // 4)
                relay(1, begin, begin + pieces // 4)
                update(1, chunks - 1, part, 4)

    @pl.when(z == 0)
    def _():
        finish_sends(0, origin_copy)

    @pl.when(active & first_chip)
    def _():
        @pl.when((z < last) | both)
        def _():
            finish_guests()

    @pl.when((z == 1) & (z < last) & (chip > 0))
    def _():
        for i in range(guests):
            guest_in(i).wait_send()

    @pl.when(active & (z < last))
    def _():
        finish_sends(0, relay_copy)

        @pl.when(z == 1)
        def _():
            finish_sends(1, origin_copy)

        @pl.when(both)
        def _():
            finish_sends(1, relay_copy)

    @pl.when(first_chip)
    def _():
        for k in range(2):
            @pl.when(z < last)
            def _():
                pivot_send(k, z + 1, p_send.at[k, z]).wait_send()

            @pl.when(z - 1 > k)
            def _():
                pivot_send(k, z - 1, p_up.at[k]).wait_send()

            finish_pivot(k)

    @pl.when(first_chip & (z == 1))
    def _():
        pivot_own(1).wait()

    for k in range(2):
        @pl.when(z > k)
        def _():
            lower_pass(k).wait_send()

            @pl.when(first_chip)
            def _():
                for target in range(n_chip - 1, 0, -1):
                    lower_send(k, target).wait_send()
                if k == 0:
                    swap_columns().wait_send()


def per_device(n_row, n_col, matrix, pivot_inverse, row_live, col_live):
    rows, columns = matrix.shape
    panels, rows_own, width = pivot_inverse.shape
    chunk = min(CHUNK, width)
    chunks = columns // chunk
    steps = chunks * PIECES
    n_chip = n_col // CORES
    guests = max(1, GUESTS // n_chip)
    f32, bf16, dma = jnp.float32, jnp.bfloat16, pltpu.SemaphoreType.DMA
    return pl.pallas_call(
        functools.partial(kernel, n_row, n_col, chunk),
        out_shape=pltpu.VMEM((rows, columns), f32),
        in_specs=[pl.BlockSpec(memory_space=pltpu.HBM)] * 4,
        out_specs=pl.BlockSpec(memory_space=pltpu.VMEM),
        scratch_shapes=[
            pltpu.SMEM(row_live.shape, jnp.int32),
            pltpu.SMEM(col_live.shape, jnp.int32),
            pltpu.VMEM((panels, chunks, width, chunk), f32),
            pltpu.VMEM((panels, width, width), f32),
            pltpu.VMEM((CORES, width // CORES, width), f32),
            pltpu.VMEM((n_chip, guests, width // PIECES, chunk), f32),
            pltpu.VMEM((panels, width, width), f32),
            pltpu.VMEM((panels, width, width), bf16),
            pltpu.VMEM((panels, width, width), bf16),
            pltpu.VMEM((width, chunk), bf16),
            pltpu.VMEM((width, chunk), bf16),
            dma, dma((2,)),
            dma((panels, steps)), dma((panels, steps)),
            dma((panels, n_row)), dma((panels, n_row)), dma((panels, n_row)), dma((panels, n_row)),
            dma((panels,)), dma, dma, dma, dma, dma,
            dma((panels, n_col // CORES)), dma((panels,)), dma((panels,)), dma((panels,)),
            dma((panels,)), dma((guests,)), dma((n_chip, guests)), dma((n_chip, guests)), dma((n_chip, guests)),
        ],
        compiler_params=pltpu.CompilerParams(
            collective_id=0, has_side_effects=True, vmem_limit_bytes=GRANT - 4 * rows * columns
        ),
    )(row_live, col_live, matrix, pivot_inverse)


def solution(mesh):
    n_row, n_col = mesh.shape["prow"], mesh.shape["pcol"]
    return jax.shard_map(
        functools.partial(per_device, n_row, n_col),
        mesh=mesh,
        in_specs=(P("prow", "pcol"), P(None, "prow", None), P(), P()),
        out_specs=P("prow", "pcol"),
        check_vma=False,
    )
```

```python
import functools

import jax
import jax.numpy as jnp
from jax import lax
from jax.experimental import pallas as pl
from jax.experimental.pallas import tpu as pltpu
from jax.sharding import PartitionSpec as P

MESH = pl.DeviceIdType.MESH
CORES = 2
CHUNK = 256
PIECES = 16
TAIL = 4
GUESTS = 32
GRANT = 67_043_328


def split(x):
    high = x.astype(jnp.bfloat16)
    return high, (x - high.astype(jnp.float32)).astype(jnp.bfloat16)


def product(left_high, left_low, right_high, right_low):
    dot = functools.partial(jnp.dot, preferred_element_type=jnp.float32)
    return dot(left_high, right_high) + (dot(left_high, right_low) + dot(left_low, right_high))


def kernel(
    n_row, n_col, chunk, row_hbm, col_hbm, mat, piv, acc,
    row_smem, col_smem, u, p, a, guest, low, low_high, low_rest, u_high, u_rest,
    acc_sem, mask_sem, u_send, u_recv, p_send, p_recv, p_pass, p_passed, p_own,
    a_own, a_send, a_recv, t_send, t_recv, l_send, l_recv, l_pass, l_passed,
    p_up, g_in, g_recv, g_down, g_out,
):
    z, pcol = lax.axis_index("prow"), lax.axis_index("pcol")
    core, chip = lax.rem(pcol, CORES), lax.div(pcol, CORES)
    n_chip = n_col // CORES
    partner = (z, pcol + 1 - 2 * core)
    width, half = piv.shape[2], piv.shape[2] // CORES
    rows_own = piv.shape[1]
    rows_half = rows_own // CORES
    chunks = acc.shape[1] // chunk
    per_block = width // chunk
    pieces = u_send.shape[1] // chunks
    piece = width // pieces
    steps = chunks * pieces
    last = n_row - 1
    guests = guest.shape[1]
    guest_start = (chunks - 2) * pieces
    first_chip, active, both = chip == 0, z > 0, z > 1
    guest_end = guest_start + jnp.where(chip > 0, guests, 0)

    def remote(src, dst, send, recv, to):
        return pltpu.make_async_remote_copy(
            src_ref=src, dst_ref=dst, send_sem=send, recv_sem=recv, device_id=to, device_id_type=MESH
        )

    masks = [
        pltpu.make_async_copy(row_hbm, row_smem, mask_sem.at[0]),
        pltpu.make_async_copy(col_hbm, col_smem, mask_sem.at[1]),
    ]

    def columns_of(j):
        start = j * chunk
        return pl.ds(start if isinstance(j, int) else pl.multiple_of(start, 128), chunk)

    def load(j):
        return pltpu.make_async_copy(mat.at[:, columns_of(j)], acc.at[:, columns_of(j)], acc_sem.at[j])

    def pivot_own(k):
        return pltpu.make_async_copy(piv.at[k], p.at[k, pl.ds(z * rows_own, rows_own)], p_own.at[k])

    def pivot_rows(k, source):
        return p.at[k, pl.ds(pl.multiple_of(source * rows_own + core * rows_half, 8), rows_half)]

    def pivot_send(k, target, send):
        return remote(
            piv.at[k, pl.ds(pl.multiple_of(core * rows_half, 8), rows_half)],
            pivot_rows(k, z), send, p_recv.at[k, z], (target, pcol),
        )

    def pivot_relay(k, source, target):
        return remote(pivot_rows(k, source), pivot_rows(k, source), p_send.at[k, source], p_recv.at[k, source], (target, pcol))

    def pivot_landed(k, source):
        return remote(pivot_rows(k, source), pivot_rows(k, source), p_send.at[k, source], p_recv.at[k, source], (z, pcol))

    def pivot_pass(k, source):
        return remote(pivot_rows(k, source), pivot_rows(k, source), p_pass.at[k, source], p_passed.at[k, source], partner)

    def piece_of(ref, j, r):
        return ref.at[j, pl.ds(pl.multiple_of(r * piece, 8), piece)]

    def relay_copy(k, s):
        place = piece_of(u.at[k], s // pieces, s % pieces)
        return remote(place, place, u_send.at[k, s], u_recv.at[k, s], (z + 1, pcol))

    def origin_copy(k, s):
        j, r = s // pieces, s % pieces
        rows = pl.ds(pl.multiple_of(r * piece, 8), piece)
        return remote(acc.at[rows, columns_of(j)], piece_of(u.at[k], j, r), u_send.at[k, s], u_recv.at[k, s], (z + 1, pcol))

    def start_of(k):
        return jnp.where(pcol <= k, per_block * pieces, 0)

    def relay(k, begin, end):
        def body(s, carry):
            copy = relay_copy(k, s)
            copy.wait_recv()

            @pl.when(z < last)
            def _():
                copy.start()

            return carry

        lax.fori_loop(jnp.maximum(begin, start_of(k)), end, body, 0)

    def originate(k, begin, end):
        def body(s, carry):
            origin_copy(k, s).start()
            return carry

        lax.fori_loop(jnp.maximum(begin, start_of(k)), end, body, 0)

    def finish_sends(k, copy):
        def body(s, carry):
            copy(k, s).wait_send()
            return carry

        if k:
            lax.fori_loop(start_of(k), guest_start, body, 0)
            lax.fori_loop(guest_end, steps, body, 0)
        else:
            lax.fori_loop(start_of(k), steps, body, 0)

    def guest_in(i):
        rows = pl.ds(i * piece, piece)
        source = acc.at[rows, columns_of(guest_start // pieces)]
        return remote(source, guest.at[chip, i], g_in.at[i], g_recv.at[chip, i], (z, core))

    def guest_down(q, i):
        return remote(guest.at[q, i], guest.at[q, i], g_down.at[q, i], g_recv.at[q, i], (z + 1, pcol))

    def guest_out(q, i):
        target = piece_of(u.at[1], guest_start // pieces, i)
        return remote(guest.at[q, i], target, g_out.at[q, i], u_recv.at[1, guest_start + i], (z, q * CORES + core))

    def pass_guests():
        def body(t, carry):
            q, i = 1 + t // guests, t % guests
            guest_down(q, i).wait_recv()

            @pl.when(z < last)
            def _():
                guest_down(q, i).start()

            @pl.when(both)
            def _():
                guest_out(q, i).start()

            return carry

        lax.fori_loop(0, (n_chip - 1) * guests, body, 0)

    def finish_guests():
        def body(t, carry):
            q, i = 1 + t // guests, t % guests

            @pl.when(z < last)
            def _():
                guest_down(q, i).wait_send()

            @pl.when(both)
            def _():
                guest_out(q, i).wait_send()

            return carry

        lax.fori_loop(0, (n_chip - 1) * guests, body, 0)

    def own_rows():
        return pl.ds(pl.multiple_of(core * half, 8), half)

    def lower_send(k, target):
        rows = low.at[k, own_rows()]
        return remote(rows, rows, l_send.at[k, target], l_recv.at[k], (z, target * CORES + core))

    def lower_pass(k):
        rows = low.at[k, own_rows()]
        return remote(rows, rows, l_pass.at[k], l_passed.at[k], partner)

    def row_mask(k):
        return row_smem[k, z].astype(jnp.float32)

    def for_sources(k, visit):
        for distance in range(1, n_row):
            @pl.when(z - distance >= 0)
            def _():
                visit(z - distance, z + 1, z < last, z > k)

            @pl.when((z + distance <= last) & (z > k))
            def _():
                visit(z + distance, z - 1, z - 1 > k, z > k)

    def relay_pivot(k):
        def visit(source, target, onward, used):
            pivot_landed(k, source).wait_recv()

            @pl.when(onward)
            def _():
                pivot_relay(k, source, target).start()

            @pl.when(used)
            def _():
                pivot_pass(k, source).start()

        for_sources(k, visit)

    def gather_pivot(k):
        pivot_own(k).wait()
        for source in range(n_row):
            @pl.when(z != source)
            def _():
                pivot_pass(k, source).wait_recv()

    def finish_pivot(k):
        def visit(source, target, onward, used):
            @pl.when(onward)
            def _():
                pivot_relay(k, source, target).wait_send()

            @pl.when(used)
            def _():
                pivot_pass(k, source).wait_send()

        for_sources(k, visit)

    def apply_pivot(k, left):
        left_high, left_low = split(left)
        for q in range(per_block):
            columns = pl.ds(q * chunk, chunk)
            right = split(p[k, :, columns])
            low[k, own_rows(), columns] = row_mask(k) * product(left_high, left_low, *right)
        for target in range(n_chip - 1, 0, -1):
            lower_send(k, target).start()
        lower_pass(k).start()

    def take_lower(k):
        @pl.when(chip > 0)
        def _():
            lower_send(k, 0).wait_recv()
            lower_pass(k).start()

        lower_pass(k).wait_recv()
        low_high[k], low_rest[k] = split(low[k])

    def update(k, j, part=0, parts=1):
        live = col_smem[k, pcol + (j // per_block) * n_col].astype(jnp.float32)

        def run():
            depth = pl.ds(part * (width // parts), width // parts)
            u_high[depth], u_rest[depth] = split(u[k, j, depth])
            for t in range(CORES):
                rows = pl.ds(t * half, half)
                left = low_high[k, rows, depth], low_rest[k, rows, depth]
                acc[rows, columns_of(j)] -= live * product(*left, u_high[depth], u_rest[depth])

        if j < per_block:
            pl.when(pcol > k)(run)
        else:
            run()

    def store_lower(k):
        @pl.when(pcol == k)
        def _():
            acc[:, pl.ds(0, width)] = low[k]

    barrier = pltpu.get_barrier_semaphore()
    relays_guests = (z == 1) & (z < last)

    def greet(condition, device):
        @pl.when(condition)
        def _():
            pl.semaphore_signal(barrier, inc=1, device_id=device, device_id_type=MESH)

    greet(active, (z - 1, pcol))
    greet(active, partner)
    greet(active & (z < last) & first_chip, (z + 1, pcol))
    greet(active & (chip > 0), (z, core))
    for other in range(1, n_chip):
        greet(relays_guests & first_chip, (z, other * CORES + core))

    for j in range(chunks):
        load(j).start()
    for copy in masks:
        copy.start()

    @pl.when(first_chip & active)
    def _():
        for k in range(2):
            pivot_own(k).start()
        pltpu.make_async_copy(mat.at[own_rows(), pl.ds(0, width)], a.at[core], a_own).start()

    targets = (
        jnp.where(z < last, 1, 0)
        + jnp.where(active, 1, 0)
        + jnp.where(both & first_chip, 1, 0)
        + jnp.where(active & first_chip, n_chip - 1, 0)
        + jnp.where(relays_guests & (chip > 0), 1, 0)
    )
    pl.semaphore_wait(barrier, targets)

    def swap_columns():
        source = mat.at[pl.ds(pl.multiple_of((1 - core) * half, 8), half), pl.ds(0, width)]
        return remote(source, a.at[core], a_send, a_recv, partner)

    def swapped_columns():
        return remote(a.at[1 - core], a.at[1 - core], a_send, a_recv, partner)

    @pl.when(first_chip)
    def _():
        for k in range(2):
            @pl.when(z < last)
            def _():
                pivot_send(k, z + 1, p_send.at[k, z]).start()

            @pl.when(z - 1 > k)
            def _():
                pivot_send(k, z - 1, p_up.at[k]).start()

        @pl.when(active)
        def _():
            swap_columns().start()

    for j in range(chunks):
        load(j).wait()

        @pl.when(z == 0)
        def _():
            originate(0, j * pieces, (j + 1) * pieces)

    for copy in masks:
        copy.wait()

    @pl.when(active)
    def _():
        @pl.when(first_chip)
        def _():
            relay_pivot(0)
            gather_pivot(0)
            pltpu.make_async_copy(mat.at[own_rows(), pl.ds(0, width)], a.at[core], a_own).wait()
            swapped_columns().wait_recv()
            apply_pivot(0, a[0])
            relay_pivot(1)

        ahead = jnp.where(pcol == 0, steps - TAIL, per_block * pieces)
        relay(0, 0, ahead)

        @pl.when(first_chip & both)
        def _():
            top = u.at[0, pl.ds(0, per_block)]
            copy = remote(top, top, t_send, t_recv, partner)

            @pl.when(core == 1)
            def _():
                copy.start()

            gather_pivot(1)

            @pl.when(core == 0)
            def _():
                copy.wait_recv()

            live = col_smem[0, 1].astype(jnp.float32)
            left = split(low[0, own_rows()])
            for q in range(per_block):
                columns = pl.ds(q * chunk, chunk)
                a[1, :, columns] -= live * product(*left, *split(u[0, q]))
            apply_pivot(1, a[1])

            @pl.when(core == 1)
            def _():
                copy.wait_send()

        relay(0, ahead, steps - TAIL)
        take_lower(0)
        for j in range(chunks - 1):
            update(0, j)
            relay(0, steps - TAIL + j, steps - TAIL + j + 1)
        relay(0, steps - TAIL + chunks - 1, steps)

        @pl.when(z == 1)
        def _():
            @pl.when(z < last)
            def _():
                @pl.when(chip > 0)
                def _():
                    for i in range(guests):
                        guest_in(i).start()

                originate(1, 0, guest_start)
                originate(1, guest_end, steps - pieces)

                @pl.when(first_chip)
                def _():
                    pass_guests()

            update(0, chunks - 1)

            @pl.when(z < last)
            def _():
                originate(1, steps - pieces, steps)

            store_lower(0)

        @pl.when(both)
        def _():
            relay(1, 0, pieces)
            update(0, chunks - 1)
            relay(1, pieces, guest_start)
            take_lower(1)
            update(1, 0)
            relay(1, guest_end, guest_end + 4)
            update(1, 1)
            store_lower(0)
            store_lower(1)
            relay(1, guest_end + 4, steps - pieces)

            @pl.when(first_chip)
            def _():
                pass_guests()

            @pl.when(chip > 0)
            def _():
                for i in range(guests):
                    relay_copy(1, guest_start + i).wait_recv()

            for j in range(2, chunks - 1):
                update(1, j)
            for part in range(4):
                begin = steps - pieces + part * (pieces // 4)
                relay(1, begin, begin + pieces // 4)
                update(1, chunks - 1, part, 4)

    @pl.when(z == 0)
    def _():
        finish_sends(0, origin_copy)

    @pl.when(active & first_chip)
    def _():
        @pl.when((z < last) | both)
        def _():
            finish_guests()

    @pl.when((z == 1) & (z < last) & (chip > 0))
    def _():
        for i in range(guests):
            guest_in(i).wait_send()

    @pl.when(active & (z < last))
    def _():
        finish_sends(0, relay_copy)

        @pl.when(z == 1)
        def _():
            finish_sends(1, origin_copy)

        @pl.when(both)
        def _():
            finish_sends(1, relay_copy)

    @pl.when(first_chip)
    def _():
        for k in range(2):
            @pl.when(z < last)
            def _():
                pivot_send(k, z + 1, p_send.at[k, z]).wait_send()

            @pl.when(z - 1 > k)
            def _():
                pivot_send(k, z - 1, p_up.at[k]).wait_send()

            finish_pivot(k)

    @pl.when(first_chip & (z == 1))
    def _():
        pivot_own(1).wait()

    for k in range(2):
        @pl.when(z > k)
        def _():
            lower_pass(k).wait_send()

            @pl.when(first_chip)
            def _():
                for target in range(n_chip - 1, 0, -1):
                    lower_send(k, target).wait_send()
                if k == 0:
                    swap_columns().wait_send()


def per_device(n_row, n_col, matrix, pivot_inverse, row_live, col_live):
    rows, columns = matrix.shape
    panels, rows_own, width = pivot_inverse.shape
    chunk = min(CHUNK, width)
    chunks = columns // chunk
    steps = chunks * PIECES
    n_chip = n_col // CORES
    guests = max(1, GUESTS // n_chip)
    f32, bf16, dma = jnp.float32, jnp.bfloat16, pltpu.SemaphoreType.DMA
    return pl.pallas_call(
        functools.partial(kernel, n_row, n_col, chunk),
        out_shape=pltpu.VMEM((rows, columns), f32),
        in_specs=[pl.BlockSpec(memory_space=pltpu.HBM)] * 4,
        out_specs=pl.BlockSpec(memory_space=pltpu.VMEM),
        scratch_shapes=[
            pltpu.SMEM(row_live.shape, jnp.int32),
            pltpu.SMEM(col_live.shape, jnp.int32),
            pltpu.VMEM((panels, chunks, width, chunk), f32),
            pltpu.VMEM((panels, width, width), f32),
            pltpu.VMEM((CORES, width // CORES, width), f32),
            pltpu.VMEM((n_chip, guests, width // PIECES, chunk), f32),
            pltpu.VMEM((panels, width, width), f32),
            pltpu.VMEM((panels, width, width), bf16),
            pltpu.VMEM((panels, width, width), bf16),
            pltpu.VMEM((width, chunk), bf16),
            pltpu.VMEM((width, chunk), bf16),
            dma((chunks,)), dma((2,)),
            dma((panels, steps)), dma((panels, steps)),
            dma((panels, n_row)), dma((panels, n_row)), dma((panels, n_row)), dma((panels, n_row)),
            dma((panels,)), dma, dma, dma, dma, dma,
            dma((panels, n_col // CORES)), dma((panels,)), dma((panels,)), dma((panels,)),
            dma((panels,)), dma((guests,)), dma((n_chip, guests)), dma((n_chip, guests)), dma((n_chip, guests)),
        ],
        compiler_params=pltpu.CompilerParams(
            collective_id=0, has_side_effects=True, vmem_limit_bytes=GRANT - 4 * rows * columns
        ),
    )(row_live, col_live, matrix, pivot_inverse)


def solution(mesh):
    n_row, n_col = mesh.shape["prow"], mesh.shape["pcol"]
    return jax.shard_map(
        functools.partial(per_device, n_row, n_col),
        mesh=mesh,
        in_specs=(P("prow", "pcol"), P(None, "prow", None), P(), P()),
        out_specs=P("prow", "pcol"),
        check_vma=False,
    )
```

```python
import functools

import jax
import jax.numpy as jnp
from jax import lax
from jax.experimental import pallas as pl
from jax.experimental.pallas import tpu as pltpu
from jax.sharding import PartitionSpec as P

MESH = pl.DeviceIdType.MESH
CORES = 2
CHUNK = 256
PIECES = 16
TAIL = 4
GUESTS = 44
FEWER = 20
GRANT = 67_043_328


def split(x):
    high = x.astype(jnp.bfloat16)
    return high, (x - high.astype(jnp.float32)).astype(jnp.bfloat16)


def product(left_high, left_low, right_high, right_low):
    dot = functools.partial(jnp.dot, preferred_element_type=jnp.float32)
    return dot(left_high, right_high) + (dot(left_high, right_low) + dot(left_low, right_high))


def kernel(
    n_row, n_col, chunk, row_hbm, col_hbm, mat, piv, acc,
    row_smem, col_smem, u, p, a, guest, low, low_high, low_rest, u_high, u_rest,
    acc_sem, mask_sem, u_send, u_recv, p_send, p_recv, p_pass, p_passed, p_own,
    a_own, a_send, a_recv, t_send, t_recv, l_send, l_recv, l_pass, l_passed,
    p_up, g_in, g_recv, g_down, g_out,
):
    z, pcol = lax.axis_index("prow"), lax.axis_index("pcol")
    core, chip = lax.rem(pcol, CORES), lax.div(pcol, CORES)
    n_chip = n_col // CORES
    partner = (z, pcol + 1 - 2 * core)
    width, half = piv.shape[2], piv.shape[2] // CORES
    rows_own = piv.shape[1]
    rows_half = rows_own // CORES
    chunks = acc.shape[1] // chunk
    per_block = width // chunk
    pieces = u_send.shape[1] // chunks
    piece = width // pieces
    steps = chunks * pieces
    last = n_row - 1
    guests = guest.shape[1] - core * (FEWER // n_chip)
    guest_start = (chunks - 2) * pieces
    first_chip, active, both = chip == 0, z > 0, z > 1
    guest_end = guest_start + jnp.where(chip > 0, guests, 0)

    def remote(src, dst, send, recv, to):
        return pltpu.make_async_remote_copy(
            src_ref=src, dst_ref=dst, send_sem=send, recv_sem=recv, device_id=to, device_id_type=MESH
        )

    masks = [
        pltpu.make_async_copy(row_hbm, row_smem, mask_sem.at[0]),
        pltpu.make_async_copy(col_hbm, col_smem, mask_sem.at[1]),
    ]

    def columns_of(j):
        start = j * chunk
        return pl.ds(start if isinstance(j, int) else pl.multiple_of(start, 128), chunk)

    def load(j):
        return pltpu.make_async_copy(mat.at[:, columns_of(j)], acc.at[:, columns_of(j)], acc_sem.at[j])

    def pivot_own(k):
        return pltpu.make_async_copy(piv.at[k], p.at[k, pl.ds(z * rows_own, rows_own)], p_own.at[k])

    def pivot_rows(k, source):
        return p.at[k, pl.ds(pl.multiple_of(source * rows_own + core * rows_half, 8), rows_half)]

    def pivot_send(k, target, send):
        return remote(
            piv.at[k, pl.ds(pl.multiple_of(core * rows_half, 8), rows_half)],
            pivot_rows(k, z), send, p_recv.at[k, z], (target, pcol),
        )

    def pivot_relay(k, source, target):
        return remote(pivot_rows(k, source), pivot_rows(k, source), p_send.at[k, source], p_recv.at[k, source], (target, pcol))

    def pivot_landed(k, source):
        return remote(pivot_rows(k, source), pivot_rows(k, source), p_send.at[k, source], p_recv.at[k, source], (z, pcol))

    def pivot_pass(k, source):
        return remote(pivot_rows(k, source), pivot_rows(k, source), p_pass.at[k, source], p_passed.at[k, source], partner)

    def piece_of(ref, j, r):
        return ref.at[j, pl.ds(pl.multiple_of(r * piece, 8), piece)]

    def relay_copy(k, s):
        place = piece_of(u.at[k], s // pieces, s % pieces)
        return remote(place, place, u_send.at[k, s], u_recv.at[k, s], (z + 1, pcol))

    def origin_copy(k, s):
        j, r = s // pieces, s % pieces
        rows = pl.ds(pl.multiple_of(r * piece, 8), piece)
        return remote(acc.at[rows, columns_of(j)], piece_of(u.at[k], j, r), u_send.at[k, s], u_recv.at[k, s], (z + 1, pcol))

    def start_of(k):
        return jnp.where(pcol <= k, per_block * pieces, 0)

    def relay(k, begin, end):
        def body(s, carry):
            copy = relay_copy(k, s)
            copy.wait_recv()

            @pl.when(z < last)
            def _():
                copy.start()

            return carry

        lax.fori_loop(jnp.maximum(begin, start_of(k)), end, body, 0)

    def originate(k, begin, end):
        def body(s, carry):
            origin_copy(k, s).start()
            return carry

        lax.fori_loop(jnp.maximum(begin, start_of(k)), end, body, 0)

    def finish_sends(k, copy):
        def body(s, carry):
            copy(k, s).wait_send()
            return carry

        if k:
            lax.fori_loop(start_of(k), guest_start, body, 0)
            lax.fori_loop(guest_end, steps, body, 0)
        else:
            lax.fori_loop(start_of(k), steps, body, 0)

    def guest_in(i):
        rows = pl.ds(pl.multiple_of(i * piece, 8), piece)
        source = acc.at[rows, columns_of(guest_start // pieces)]
        return remote(source, guest.at[chip, i], g_in.at[i], g_recv.at[chip, i], (z, core))

    def guest_down(q, i):
        return remote(guest.at[q, i], guest.at[q, i], g_down.at[q, i], g_recv.at[q, i], (z + 1, pcol))

    def guest_out(q, i):
        target = piece_of(u.at[1], guest_start // pieces, i)
        return remote(guest.at[q, i], target, g_out.at[q, i], u_recv.at[1, guest_start + i], (z, q * CORES + core))

    def pass_guests():
        def body(i, carry):
            for q in range(1, n_chip):
                guest_down(q, i).wait_recv()

                @pl.when(z < last)
                def _():
                    guest_down(q, i).start()

                @pl.when(both)
                def _():
                    guest_out(q, i).start()

            return carry

        lax.fori_loop(0, guests, body, 0)

    def finish_guests():
        def body(i, carry):
            for q in range(1, n_chip):
                @pl.when(z < last)
                def _():
                    guest_down(q, i).wait_send()

                @pl.when(both)
                def _():
                    guest_out(q, i).wait_send()

            return carry

        lax.fori_loop(0, guests, body, 0)

    def each_guest(act):
        def body(i, carry):
            act(i)
            return carry

        lax.fori_loop(0, guests, body, 0)

    def own_rows():
        return pl.ds(pl.multiple_of(core * half, 8), half)

    def lower_send(k, target):
        rows = low.at[k, own_rows()]
        return remote(rows, rows, l_send.at[k, target], l_recv.at[k], (z, target * CORES + core))

    def lower_pass(k):
        rows = low.at[k, own_rows()]
        return remote(rows, rows, l_pass.at[k], l_passed.at[k], partner)

    def row_mask(k):
        return row_smem[k, z].astype(jnp.float32)

    def for_sources(k, visit):
        for distance in range(1, n_row):
            @pl.when(z - distance >= 0)
            def _():
                visit(z - distance, z + 1, z < last, z > k)

            @pl.when((z + distance <= last) & (z > k))
            def _():
                visit(z + distance, z - 1, z - 1 > k, z > k)

    def relay_pivot(k):
        def visit(source, target, onward, used):
            pivot_landed(k, source).wait_recv()

            @pl.when(onward)
            def _():
                pivot_relay(k, source, target).start()

            @pl.when(used)
            def _():
                pivot_pass(k, source).start()

        for_sources(k, visit)

    def gather_pivot(k):
        pivot_own(k).wait()
        for source in range(n_row):
            @pl.when(z != source)
            def _():
                pivot_pass(k, source).wait_recv()

    def finish_pivot(k):
        def visit(source, target, onward, used):
            @pl.when(onward)
            def _():
                pivot_relay(k, source, target).wait_send()

            @pl.when(used)
            def _():
                pivot_pass(k, source).wait_send()

        for_sources(k, visit)

    def apply_pivot(k, left):
        left_high, left_low = split(left)
        for q in range(per_block):
            columns = pl.ds(q * chunk, chunk)
            right = split(p[k, :, columns])
            low[k, own_rows(), columns] = row_mask(k) * product(left_high, left_low, *right)
        for target in range(n_chip - 1, 0, -1):
            lower_send(k, target).start()
        lower_pass(k).start()

    def take_lower(k):
        @pl.when(chip > 0)
        def _():
            lower_send(k, 0).wait_recv()
            lower_pass(k).start()

        lower_pass(k).wait_recv()
        low_high[k], low_rest[k] = split(low[k])

    def update(k, j, part=0, parts=1):
        live = col_smem[k, pcol + (j // per_block) * n_col].astype(jnp.float32)

        def run():
            depth = pl.ds(part * (width // parts), width // parts)
            u_high[depth], u_rest[depth] = split(u[k, j, depth])
            for t in range(CORES):
                rows = pl.ds(t * half, half)
                left = low_high[k, rows, depth], low_rest[k, rows, depth]
                acc[rows, columns_of(j)] -= live * product(*left, u_high[depth], u_rest[depth])

        if j < per_block:
            pl.when(pcol > k)(run)
        else:
            run()

    def store_lower(k):
        @pl.when(pcol == k)
        def _():
            acc[:, pl.ds(0, width)] = low[k]

    barrier = pltpu.get_barrier_semaphore()
    relays_guests = (z == 1) & (z < last)

    def greet(condition, device):
        @pl.when(condition)
        def _():
            pl.semaphore_signal(barrier, inc=1, device_id=device, device_id_type=MESH)

    greet(active, (z - 1, pcol))
    greet(active, partner)
    greet(active & (z < last) & first_chip, (z + 1, pcol))
    greet(active & (chip > 0), (z, core))
    for other in range(1, n_chip):
        greet(relays_guests & first_chip, (z, other * CORES + core))

    for j in range(chunks):
        load(j).start()
    for copy in masks:
        copy.start()

    @pl.when(first_chip & active)
    def _():
        for k in range(2):
            pivot_own(k).start()
        pltpu.make_async_copy(mat.at[own_rows(), pl.ds(0, width)], a.at[core], a_own).start()

    targets = (
        jnp.where(z < last, 1, 0)
        + jnp.where(active, 1, 0)
        + jnp.where(both & first_chip, 1, 0)
        + jnp.where(active & first_chip, n_chip - 1, 0)
        + jnp.where(relays_guests & (chip > 0), 1, 0)
    )
    pl.semaphore_wait(barrier, targets)

    def swap_columns():
        source = mat.at[pl.ds(pl.multiple_of((1 - core) * half, 8), half), pl.ds(0, width)]
        return remote(source, a.at[core], a_send, a_recv, partner)

    def swapped_columns():
        return remote(a.at[1 - core], a.at[1 - core], a_send, a_recv, partner)

    @pl.when(first_chip)
    def _():
        for k in range(2):
            @pl.when(z < last)
            def _():
                pivot_send(k, z + 1, p_send.at[k, z]).start()

            @pl.when(z - 1 > k)
            def _():
                pivot_send(k, z - 1, p_up.at[k]).start()

        @pl.when(active)
        def _():
            swap_columns().start()

    for j in range(chunks):
        load(j).wait()

        @pl.when(z == 0)
        def _():
            originate(0, j * pieces, (j + 1) * pieces)

    for copy in masks:
        copy.wait()

    @pl.when(active)
    def _():
        @pl.when(first_chip)
        def _():
            relay_pivot(0)
            gather_pivot(0)
            pltpu.make_async_copy(mat.at[own_rows(), pl.ds(0, width)], a.at[core], a_own).wait()
            swapped_columns().wait_recv()
            apply_pivot(0, a[0])
            relay_pivot(1)

        ahead = jnp.where(pcol == 0, steps - TAIL, per_block * pieces)
        relay(0, 0, ahead)

        @pl.when(first_chip & both)
        def _():
            top = u.at[0, pl.ds(0, per_block)]
            copy = remote(top, top, t_send, t_recv, partner)

            @pl.when(core == 1)
            def _():
                copy.start()

            gather_pivot(1)

            @pl.when(core == 0)
            def _():
                copy.wait_recv()

            live = col_smem[0, 1].astype(jnp.float32)
            left = split(low[0, own_rows()])
            for q in range(per_block):
                columns = pl.ds(q * chunk, chunk)
                a[1, :, columns] -= live * product(*left, *split(u[0, q]))
            apply_pivot(1, a[1])

            @pl.when(core == 1)
            def _():
                copy.wait_send()

        relay(0, ahead, steps - TAIL)
        take_lower(0)
        for j in range(chunks - 1):
            update(0, j)
            relay(0, steps - TAIL + j, steps - TAIL + j + 1)
        relay(0, steps - TAIL + chunks - 1, steps)

        @pl.when(z == 1)
        def _():
            @pl.when(z < last)
            def _():
                @pl.when(chip > 0)
                def _():
                    each_guest(lambda i: guest_in(i).start())

                originate(1, 0, guest_start)
                originate(1, guest_end, steps - pieces)

                @pl.when(first_chip)
                def _():
                    pass_guests()

            update(0, chunks - 1)

            @pl.when(z < last)
            def _():
                originate(1, steps - pieces, steps)

            store_lower(0)

        @pl.when(both)
        def _():
            relay(1, 0, pieces)
            update(0, chunks - 1)
            relay(1, pieces, guest_start)
            take_lower(1)
            update(1, 0)
            relay(1, guest_end, guest_end + 4)
            update(1, 1)
            store_lower(0)
            store_lower(1)
            relay(1, guest_end + 4, steps - pieces)

            @pl.when(first_chip)
            def _():
                pass_guests()

            @pl.when(chip > 0)
            def _():
                each_guest(lambda i: relay_copy(1, guest_start + i).wait_recv())

            for j in range(2, chunks - 1):
                update(1, j)
            for part in range(4):
                begin = steps - pieces + part * (pieces // 4)
                relay(1, begin, begin + pieces // 4)
                update(1, chunks - 1, part, 4)

    @pl.when(z == 0)
    def _():
        finish_sends(0, origin_copy)

    @pl.when(active & first_chip)
    def _():
        @pl.when((z < last) | both)
        def _():
            finish_guests()

    @pl.when((z == 1) & (z < last) & (chip > 0))
    def _():
        each_guest(lambda i: guest_in(i).wait_send())

    @pl.when(active & (z < last))
    def _():
        finish_sends(0, relay_copy)

        @pl.when(z == 1)
        def _():
            finish_sends(1, origin_copy)

        @pl.when(both)
        def _():
            finish_sends(1, relay_copy)

    @pl.when(first_chip)
    def _():
        for k in range(2):
            @pl.when(z < last)
            def _():
                pivot_send(k, z + 1, p_send.at[k, z]).wait_send()

            @pl.when(z - 1 > k)
            def _():
                pivot_send(k, z - 1, p_up.at[k]).wait_send()

            finish_pivot(k)

    @pl.when(first_chip & (z == 1))
    def _():
        pivot_own(1).wait()

    for k in range(2):
        @pl.when(z > k)
        def _():
            lower_pass(k).wait_send()

            @pl.when(first_chip)
            def _():
                for target in range(n_chip - 1, 0, -1):
                    lower_send(k, target).wait_send()
                if k == 0:
                    swap_columns().wait_send()


def per_device(n_row, n_col, matrix, pivot_inverse, row_live, col_live):
    rows, columns = matrix.shape
    panels, rows_own, width = pivot_inverse.shape
    chunk = min(CHUNK, width)
    chunks = columns // chunk
    steps = chunks * PIECES
    n_chip = n_col // CORES
    guests = max(1, GUESTS // n_chip)
    f32, bf16, dma = jnp.float32, jnp.bfloat16, pltpu.SemaphoreType.DMA
    return pl.pallas_call(
        functools.partial(kernel, n_row, n_col, chunk),
        out_shape=pltpu.VMEM((rows, columns), f32),
        in_specs=[pl.BlockSpec(memory_space=pltpu.HBM)] * 4,
        out_specs=pl.BlockSpec(memory_space=pltpu.VMEM),
        scratch_shapes=[
            pltpu.SMEM(row_live.shape, jnp.int32),
            pltpu.SMEM(col_live.shape, jnp.int32),
            pltpu.VMEM((panels, chunks, width, chunk), f32),
            pltpu.VMEM((panels, width, width), f32),
            pltpu.VMEM((CORES, width // CORES, width), f32),
            pltpu.VMEM((n_chip, guests, width // PIECES, chunk), f32),
            pltpu.VMEM((panels, width, width), f32),
            pltpu.VMEM((panels, width, width), bf16),
            pltpu.VMEM((panels, width, width), bf16),
            pltpu.VMEM((width, chunk), bf16),
            pltpu.VMEM((width, chunk), bf16),
            dma((chunks,)), dma((2,)),
            dma((panels, steps)), dma((panels, steps)),
            dma((panels, n_row)), dma((panels, n_row)), dma((panels, n_row)), dma((panels, n_row)),
            dma((panels,)), dma, dma, dma, dma, dma,
            dma((panels, n_col // CORES)), dma((panels,)), dma((panels,)), dma((panels,)),
            dma((panels,)), dma((guests,)), dma((n_chip, guests)), dma((n_chip, guests)), dma((n_chip, guests)),
        ],
        compiler_params=pltpu.CompilerParams(
            collective_id=0, has_side_effects=True, vmem_limit_bytes=GRANT - 4 * rows * columns
        ),
    )(row_live, col_live, matrix, pivot_inverse)


def solution(mesh):
    n_row, n_col = mesh.shape["prow"], mesh.shape["pcol"]
    return jax.shard_map(
        functools.partial(per_device, n_row, n_col),
        mesh=mesh,
        in_specs=(P("prow", "pcol"), P(None, "prow", None), P(), P()),
        out_specs=P("prow", "pcol"),
        check_vma=False,
    )
```

```python
import functools

import jax
import jax.numpy as jnp
from jax import lax
from jax.experimental import pallas as pl
from jax.experimental.pallas import tpu as pltpu
from jax.sharding import PartitionSpec as P

MESH = pl.DeviceIdType.MESH
CORES = 2
CHUNK = 256
PIECES = 16
TAIL = 4
GUESTS = 28
GRANT = 67_043_328


def split(x):
    high = x.astype(jnp.bfloat16)
    return high, (x - high.astype(jnp.float32)).astype(jnp.bfloat16)


def product(left_high, left_low, right_high, right_low):
    dot = functools.partial(jnp.dot, preferred_element_type=jnp.float32)
    return dot(left_high, right_high) + (dot(left_high, right_low) + dot(left_low, right_high))


def kernel(
    n_row, n_col, chunk, row_hbm, col_hbm, mat, piv, acc,
    row_smem, col_smem, u, p, a, guest, low, low_high, low_rest, u_high, u_rest,
    acc_sem, mask_sem, u_send, u_recv, p_send, p_recv, p_pass, p_passed, p_own,
    a_own, a_send, a_recv, t_send, t_recv, l_send, l_recv, l_pass, l_passed,
    p_up, g_in, g_recv, g_down, g_out,
):
    z, pcol = lax.axis_index("prow"), lax.axis_index("pcol")
    core, chip = lax.rem(pcol, CORES), lax.div(pcol, CORES)
    n_chip = n_col // CORES
    partner = (z, pcol + 1 - 2 * core)
    width, half = piv.shape[2], piv.shape[2] // CORES
    rows_own = piv.shape[1]
    rows_half = rows_own // CORES
    chunks = acc.shape[1] // chunk
    per_block = width // chunk
    pieces = u_send.shape[1] // chunks
    piece = width // pieces
    steps = chunks * pieces
    last = n_row - 1
    guests = guest.shape[1]
    guest_start = (chunks - 2) * pieces
    first_chip, active, both = chip == 0, z > 0, z > 1
    guest_end = guest_start + jnp.where(chip > 0, guests, 0)

    def remote(src, dst, send, recv, to):
        return pltpu.make_async_remote_copy(
            src_ref=src, dst_ref=dst, send_sem=send, recv_sem=recv, device_id=to, device_id_type=MESH
        )

    masks = [
        pltpu.make_async_copy(row_hbm, row_smem, mask_sem.at[0]),
        pltpu.make_async_copy(col_hbm, col_smem, mask_sem.at[1]),
    ]

    def columns_of(j):
        start = j * chunk
        return pl.ds(start if isinstance(j, int) else pl.multiple_of(start, 128), chunk)

    def load(j):
        return pltpu.make_async_copy(mat.at[:, columns_of(j)], acc.at[:, columns_of(j)], acc_sem.at[j])

    def pivot_own(k):
        return pltpu.make_async_copy(piv.at[k], p.at[k, pl.ds(z * rows_own, rows_own)], p_own.at[k])

    def pivot_rows(k, source):
        return p.at[k, pl.ds(pl.multiple_of(source * rows_own + core * rows_half, 8), rows_half)]

    def pivot_send(k, target, send):
        return remote(
            piv.at[k, pl.ds(pl.multiple_of(core * rows_half, 8), rows_half)],
            pivot_rows(k, z), send, p_recv.at[k, z], (target, pcol),
        )

    def pivot_relay(k, source, target):
        return remote(pivot_rows(k, source), pivot_rows(k, source), p_send.at[k, source], p_recv.at[k, source], (target, pcol))

    def pivot_landed(k, source):
        return remote(pivot_rows(k, source), pivot_rows(k, source), p_send.at[k, source], p_recv.at[k, source], (z, pcol))

    def pivot_pass(k, source):
        return remote(pivot_rows(k, source), pivot_rows(k, source), p_pass.at[k, source], p_passed.at[k, source], partner)

    def piece_of(ref, j, r):
        return ref.at[j, pl.ds(pl.multiple_of(r * piece, 8), piece)]

    def relay_copy(k, s):
        place = piece_of(u.at[k], s // pieces, s % pieces)
        return remote(place, place, u_send.at[k, s], u_recv.at[k, s], (z + 1, pcol))

    def origin_copy(k, s):
        j, r = s // pieces, s % pieces
        rows = pl.ds(pl.multiple_of(r * piece, 8), piece)
        return remote(acc.at[rows, columns_of(j)], piece_of(u.at[k], j, r), u_send.at[k, s], u_recv.at[k, s], (z + 1, pcol))

    def start_of(k):
        return jnp.where(pcol <= k, per_block * pieces, 0)

    def relay(k, begin, end):
        def body(s, carry):
            copy = relay_copy(k, s)
            copy.wait_recv()

            @pl.when(z < last)
            def _():
                copy.start()

            return carry

        lax.fori_loop(jnp.maximum(begin, start_of(k)), end, body, 0)

    def originate(k, begin, end):
        def body(s, carry):
            origin_copy(k, s).start()
            return carry

        lax.fori_loop(jnp.maximum(begin, start_of(k)), end, body, 0)

    def finish_sends(k, copy):
        def body(s, carry):
            copy(k, s).wait_send()
            return carry

        if k:
            lax.fori_loop(start_of(k), guest_start, body, 0)
            lax.fori_loop(guest_end, steps, body, 0)
        else:
            lax.fori_loop(start_of(k), steps, body, 0)

    def guest_in(i):
        rows = pl.ds(i * piece, piece)
        source = acc.at[rows, columns_of(guest_start // pieces)]
        return remote(source, guest.at[chip, i], g_in.at[i], g_recv.at[chip, i], (z, core))

    def guest_down(q, i):
        return remote(guest.at[q, i], guest.at[q, i], g_down.at[q, i], g_recv.at[q, i], (z + 1, pcol))

    def guest_out(q, i):
        target = piece_of(u.at[1], guest_start // pieces, i)
        return remote(guest.at[q, i], target, g_out.at[q, i], u_recv.at[1, guest_start + i], (z, q * CORES + core))

    def pass_guests():
        def body(t, carry):
            q, i = 1 + t // guests, t % guests
            guest_down(q, i).wait_recv()

            @pl.when(z < last)
            def _():
                guest_down(q, i).start()

            @pl.when(both)
            def _():
                guest_out(q, i).start()

            return carry

        lax.fori_loop(0, (n_chip - 1) * guests, body, 0)

    def finish_guests():
        def body(t, carry):
            q, i = 1 + t // guests, t % guests

            @pl.when(z < last)
            def _():
                guest_down(q, i).wait_send()

            @pl.when(both)
            def _():
                guest_out(q, i).wait_send()

            return carry

        lax.fori_loop(0, (n_chip - 1) * guests, body, 0)

    def own_rows():
        return pl.ds(pl.multiple_of(core * half, 8), half)

    def lower_send(k, target):
        rows = low.at[k, own_rows()]
        return remote(rows, rows, l_send.at[k, target], l_recv.at[k], (z, target * CORES + core))

    def lower_pass(k):
        rows = low.at[k, own_rows()]
        return remote(rows, rows, l_pass.at[k], l_passed.at[k], partner)

    def row_mask(k):
        return row_smem[k, z].astype(jnp.float32)

    def for_sources(k, visit):
        for distance in range(1, n_row):
            @pl.when(z - distance >= 0)
            def _():
                visit(z - distance, z + 1, z < last, z > k)

            @pl.when((z + distance <= last) & (z > k))
            def _():
                visit(z + distance, z - 1, z - 1 > k, z > k)

    def relay_pivot(k):
        def visit(source, target, onward, used):
            pivot_landed(k, source).wait_recv()

            @pl.when(onward)
            def _():
                pivot_relay(k, source, target).start()

            @pl.when(used)
            def _():
                pivot_pass(k, source).start()

        for_sources(k, visit)

    def gather_pivot(k):
        pivot_own(k).wait()
        for source in range(n_row):
            @pl.when(z != source)
            def _():
                pivot_pass(k, source).wait_recv()

    def finish_pivot(k):
        def visit(source, target, onward, used):
            @pl.when(onward)
            def _():
                pivot_relay(k, source, target).wait_send()

            @pl.when(used)
            def _():
                pivot_pass(k, source).wait_send()

        for_sources(k, visit)

    def apply_pivot(k, left):
        left_high, left_low = split(left)
        for q in range(per_block):
            columns = pl.ds(q * chunk, chunk)
            right = split(p[k, :, columns])
            low[k, own_rows(), columns] = row_mask(k) * product(left_high, left_low, *right)
        for target in range(n_chip - 1, 0, -1):
            lower_send(k, target).start()
        lower_pass(k).start()

    def take_lower(k):
        @pl.when(chip > 0)
        def _():
            lower_send(k, 0).wait_recv()
            lower_pass(k).start()

        lower_pass(k).wait_recv()
        low_high[k], low_rest[k] = split(low[k])

    def update(k, j, part=0, parts=1):
        live = col_smem[k, pcol + (j // per_block) * n_col].astype(jnp.float32)

        def run():
            depth = pl.ds(part * (width // parts), width // parts)
            u_high[depth], u_rest[depth] = split(u[k, j, depth])
            for t in range(CORES):
                rows = pl.ds(t * half, half)
                left = low_high[k, rows, depth], low_rest[k, rows, depth]
                acc[rows, columns_of(j)] -= live * product(*left, u_high[depth], u_rest[depth])

        if j < per_block:
            pl.when(pcol > k)(run)
        else:
            run()

    def store_lower(k):
        @pl.when(pcol == k)
        def _():
            acc[:, pl.ds(0, width)] = low[k]

    barrier = pltpu.get_barrier_semaphore()
    relays_guests = (z == 1) & (z < last)

    def greet(condition, device):
        @pl.when(condition)
        def _():
            pl.semaphore_signal(barrier, inc=1, device_id=device, device_id_type=MESH)

    greet(active, (z - 1, pcol))
    greet(active, partner)
    greet(active & (z < last) & first_chip, (z + 1, pcol))
    greet(active & (chip > 0), (z, core))
    for other in range(1, n_chip):
        greet(relays_guests & first_chip, (z, other * CORES + core))

    for j in range(chunks):
        load(j).start()
    for copy in masks:
        copy.start()

    @pl.when(first_chip & active)
    def _():
        for k in range(2):
            pivot_own(k).start()
        pltpu.make_async_copy(mat.at[own_rows(), pl.ds(0, width)], a.at[core], a_own).start()

    targets = (
        jnp.where(z < last, 1, 0)
        + jnp.where(active, 1, 0)
        + jnp.where(both & first_chip, 1, 0)
        + jnp.where(active & first_chip, n_chip - 1, 0)
        + jnp.where(relays_guests & (chip > 0), 1, 0)
    )
    pl.semaphore_wait(barrier, targets)

    def swap_columns():
        source = mat.at[pl.ds(pl.multiple_of((1 - core) * half, 8), half), pl.ds(0, width)]
        return remote(source, a.at[core], a_send, a_recv, partner)

    def swapped_columns():
        return remote(a.at[1 - core], a.at[1 - core], a_send, a_recv, partner)

    @pl.when(first_chip)
    def _():
        for k in range(2):
            @pl.when(z < last)
            def _():
                pivot_send(k, z + 1, p_send.at[k, z]).start()

            @pl.when(z - 1 > k)
            def _():
                pivot_send(k, z - 1, p_up.at[k]).start()

        @pl.when(active)
        def _():
            swap_columns().start()

    for j in range(chunks):
        load(j).wait()

        @pl.when(z == 0)
        def _():
            originate(0, j * pieces, (j + 1) * pieces)

    for copy in masks:
        copy.wait()

    @pl.when(active)
    def _():
        @pl.when(first_chip)
        def _():
            relay_pivot(0)
            gather_pivot(0)
            pltpu.make_async_copy(mat.at[own_rows(), pl.ds(0, width)], a.at[core], a_own).wait()
            swapped_columns().wait_recv()
            apply_pivot(0, a[0])
            relay_pivot(1)

        ahead = jnp.where(pcol == 0, steps - TAIL, per_block * pieces)
        relay(0, 0, ahead)

        @pl.when(first_chip & both)
        def _():
            top = u.at[0, pl.ds(0, per_block)]
            copy = remote(top, top, t_send, t_recv, partner)

            @pl.when(core == 1)
            def _():
                copy.start()

            gather_pivot(1)

            @pl.when(core == 0)
            def _():
                copy.wait_recv()

            live = col_smem[0, 1].astype(jnp.float32)
            left = split(low[0, own_rows()])
            for q in range(per_block):
                columns = pl.ds(q * chunk, chunk)
                a[1, :, columns] -= live * product(*left, *split(u[0, q]))
            apply_pivot(1, a[1])

            @pl.when(core == 1)
            def _():
                copy.wait_send()

        relay(0, ahead, steps - TAIL)
        take_lower(0)
        for j in range(chunks - 1):
            update(0, j)
            relay(0, steps - TAIL + j, steps - TAIL + j + 1)
        relay(0, steps - TAIL + chunks - 1, steps)

        @pl.when(z == 1)
        def _():
            @pl.when(z < last)
            def _():
                @pl.when(chip > 0)
                def _():
                    for i in range(guests):
                        guest_in(i).start()

                originate(1, 0, guest_start)
                originate(1, guest_end, steps - pieces)

                @pl.when(first_chip)
                def _():
                    pass_guests()

            update(0, chunks - 1)

            @pl.when(z < last)
            def _():
                originate(1, steps - pieces, steps)

            store_lower(0)

        @pl.when(both)
        def _():
            relay(1, 0, pieces)
            update(0, chunks - 1)
            relay(1, pieces, guest_start)
            take_lower(1)
            update(1, 0)
            relay(1, guest_end, guest_end + 4)
            update(1, 1)
            store_lower(0)
            store_lower(1)
            relay(1, guest_end + 4, steps - pieces)

            @pl.when(first_chip)
            def _():
                pass_guests()

            @pl.when(chip > 0)
            def _():
                for i in range(guests):
                    relay_copy(1, guest_start + i).wait_recv()

            for j in range(2, chunks - 1):
                update(1, j)
            for part in range(4):
                begin = steps - pieces + part * (pieces // 4)
                relay(1, begin, begin + pieces // 4)
                update(1, chunks - 1, part, 4)

    @pl.when(z == 0)
    def _():
        finish_sends(0, origin_copy)

    @pl.when(active & first_chip)
    def _():
        @pl.when((z < last) | both)
        def _():
            finish_guests()

    @pl.when((z == 1) & (z < last) & (chip > 0))
    def _():
        for i in range(guests):
            guest_in(i).wait_send()

    @pl.when(active & (z < last))
    def _():
        finish_sends(0, relay_copy)

        @pl.when(z == 1)
        def _():
            finish_sends(1, origin_copy)

        @pl.when(both)
        def _():
            finish_sends(1, relay_copy)

    @pl.when(first_chip)
    def _():
        for k in range(2):
            @pl.when(z < last)
            def _():
                pivot_send(k, z + 1, p_send.at[k, z]).wait_send()

            @pl.when(z - 1 > k)
            def _():
                pivot_send(k, z - 1, p_up.at[k]).wait_send()

            finish_pivot(k)

    @pl.when(first_chip & (z == 1))
    def _():
        pivot_own(1).wait()

    for k in range(2):
        @pl.when(z > k)
        def _():
            lower_pass(k).wait_send()

            @pl.when(first_chip)
            def _():
                for target in range(n_chip - 1, 0, -1):
                    lower_send(k, target).wait_send()
                if k == 0:
                    swap_columns().wait_send()


def per_device(n_row, n_col, matrix, pivot_inverse, row_live, col_live):
    rows, columns = matrix.shape
    panels, rows_own, width = pivot_inverse.shape
    chunk = min(CHUNK, width)
    chunks = columns // chunk
    steps = chunks * PIECES
    n_chip = n_col // CORES
    guests = max(1, GUESTS // n_chip)
    f32, bf16, dma = jnp.float32, jnp.bfloat16, pltpu.SemaphoreType.DMA
    return pl.pallas_call(
        functools.partial(kernel, n_row, n_col, chunk),
        out_shape=pltpu.VMEM((rows, columns), f32),
        in_specs=[pl.BlockSpec(memory_space=pltpu.HBM)] * 4,
        out_specs=pl.BlockSpec(memory_space=pltpu.VMEM),
        scratch_shapes=[
            pltpu.SMEM(row_live.shape, jnp.int32),
            pltpu.SMEM(col_live.shape, jnp.int32),
            pltpu.VMEM((panels, chunks, width, chunk), f32),
            pltpu.VMEM((panels, width, width), f32),
            pltpu.VMEM((CORES, width // CORES, width), f32),
            pltpu.VMEM((n_chip, guests, width // PIECES, chunk), f32),
            pltpu.VMEM((panels, width, width), f32),
            pltpu.VMEM((panels, width, width), bf16),
            pltpu.VMEM((panels, width, width), bf16),
            pltpu.VMEM((width, chunk), bf16),
            pltpu.VMEM((width, chunk), bf16),
            dma((chunks,)), dma((2,)),
            dma((panels, steps)), dma((panels, steps)),
            dma((panels, n_row)), dma((panels, n_row)), dma((panels, n_row)), dma((panels, n_row)),
            dma((panels,)), dma, dma, dma, dma, dma,
            dma((panels, n_col // CORES)), dma((panels,)), dma((panels,)), dma((panels,)),
            dma((panels,)), dma((guests,)), dma((n_chip, guests)), dma((n_chip, guests)), dma((n_chip, guests)),
        ],
        compiler_params=pltpu.CompilerParams(
            collective_id=0, has_side_effects=True, vmem_limit_bytes=GRANT - 4 * rows * columns
        ),
    )(row_live, col_live, matrix, pivot_inverse)


def solution(mesh):
    n_row, n_col = mesh.shape["prow"], mesh.shape["pcol"]
    return jax.shard_map(
        functools.partial(per_device, n_row, n_col),
        mesh=mesh,
        in_specs=(P("prow", "pcol"), P(None, "prow", None), P(), P()),
        out_specs=P("prow", "pcol"),
        check_vma=False,
    )
```
